32 devices in a mesh: parts: 2 (over x), lat: 8 (over z, y), lev: 2 (over core).
Axes of the slice: x: 2, y: 2, z: 4, core: 2. Of those that a mesh axis runs over, the one named last changes fastest.
Arguments:
- fields: float32 [5, 60, 128, 512], P(None, 'lev', ('parts', 'lat')), parts along dimension 2, may hold values from -6 to 6
- region: int32 [128, 512], P(('parts', 'lat')), parts along dimension 0, may hold values from 0 to 7
- land: int32 [128, 512], P(('parts', 'lat')), parts along dimension 0, may hold values 0 or 1
- coef_table: float32 [60, 8], replicated, may hold values from 0.02 to 0.24
- w_in: bfloat16 [1024, 300], replicated, may hold values from -0.375 to 0.375
- b_in: float32 [1024], replicated, may hold values from -3 to 3
- w_mid: bfloat16 [2, 1024, 1024], replicated, may hold values from -0.1875 to 0.1875
- b_mid: float32 [2, 1024], replicated, may hold values from -3 to 3
- w_out: bfloat16 [300, 1024], replicated, may hold values from -0.1875 to 0.1875
- b_out: float32 [300], replicated, may hold values from -3 to 3
Outputs:
- closure: float32 [5, 60, 128, 512], P(None, 'lev', ('parts', 'lat')), parts along dimension 2
The draws below stay inside these ranges and needn't reach their ends.
There are 2 independent parts, one for each index of `parts`. The reference program is written for one: setup_inputs(seed, part) draws one part's arguments, and reference() takes and returns one part's arrays. A program takes and returns all parts, laid end to end along the dimension named above; an argument that names none is the same for every part. Nothing has to cross between parts.
All inputs are finite; a program needn't handle non-finite values. No bound on the sum of `land` on one device may be relied on, other than what follows from the above.
Results may differ from the reference program's by a relative error of at most 0.0025.
Values may be sent and summed in bfloat16 or wider, within the bound.
A program may use at most 64 MiB of HBM per device.

```python
import math
import jax
import jax.numpy as jnp
from jax import lax

V = 5
L = 60
FEAT = 300
HID = 1024
MIDS = 2
REGIONS = 8
PRE = 4
POST = 2
ROWS = 8
NLON = 512
NLAT = 64
N_LAT = 8


def with_ends(values, rng, least, largest):
    place = [jax.random.randint(jax.random.fold_in(rng, axis), (), 0, length) for axis, length in enumerate(values.shape)]
    main_axis = values.shape.index(max(values.shape))
    next_to = place[:main_axis] + [(place[main_axis] + 1) % values.shape[main_axis]] + place[main_axis + 1:]
    return values.at[tuple(place)].set(least).at[tuple(next_to)].set(largest)


def steps_of(own_key, extent, pieces, low, high):
    factor_of = 1.0
    for position, parts in pieces:
        heights = jax.random.uniform(jax.random.fold_in(jax.random.fold_in(own_key, 6), position), (parts,), jnp.float32, low / len(pieces), high / len(pieces))
        factor_of = factor_of * jnp.repeat(jnp.exp(heights), extent[position] // parts).reshape((-1,) + (1,) * (len(extent) - 1 - position))
    return factor_of


def normal_values(stream_key, shape, spread, reach, split=(), held_as=jnp.bfloat16):
    array = jax.random.normal(stream_key, shape, jnp.float32) * spread
    if len(split) > 0:
        array = steps_of(stream_key, shape, split, -0.22, 0.18) * array
    return jnp.clip(array, min=-reach, max=reach).astype(held_as)


def setup_inputs(seed: int = 0, part: int = 0) -> dict:
    key_of = jax.random.split(jax.random.key(seed), 11)
    own_keys = jax.random.split(jax.random.fold_in(key_of[10], part), 11)
    return {
        "fields": normal_values(own_keys[0], (V, L, NLAT, NLON), 1.0, 6.0, ((1, 2), (2, 8)), jnp.float32),
        "region": with_ends(jax.random.randint(own_keys[1], (NLAT, NLON), 0, REGIONS), jax.random.fold_in(own_keys[1], 1), 0, REGIONS - 1).astype(jnp.int32),
        "land": with_ends((jax.random.randint(own_keys[2], (NLAT, NLON), 0, 10) < 3).astype(jnp.int32), jax.random.fold_in(own_keys[2], 1), 0, 1),
        "coef_table": jnp.clip(jnp.exp(jax.random.uniform(key_of[3], (L, REGIONS), jnp.float32, math.log(0.02), math.log(0.24))), 0.02, 0.24),
        "w_in": normal_values(key_of[4], (HID, FEAT), FEAT ** -0.5, 0.375),
        "b_in": normal_values(key_of[5], (HID,), 0.5, 3.0, (), jnp.float32),
        "w_mid": normal_values(key_of[6], (MIDS, HID, HID), HID ** -0.5, 0.1875),
        "b_mid": normal_values(key_of[7], (MIDS, HID), 0.5, 3.0, (), jnp.float32),
        "w_out": normal_values(key_of[8], (FEAT, HID), HID ** -0.5, 0.1875),
        "b_out": normal_values(key_of[9], (FEAT,), 0.5, 3.0, (), jnp.float32),
    }


def diffuse(fields, coeffs):
    east_face = jnp.sqrt(coeffs * jnp.roll(coeffs, -1, axis=2))
    east_flux = east_face * (jnp.roll(fields, -1, axis=3) - fields)
    zonal = east_flux - jnp.roll(east_flux, 1, axis=3)
    north_face = jnp.sqrt(coeffs[:, :-1] * coeffs[:, 1:])
    north_flux = north_face * (fields[:, :, 1:] - fields[:, :, :-1])
    meridional = north_flux[:, :, 1:] - north_flux[:, :, :-1]
    return fields[:, :, 1:-1] + zonal[:, :, 1:-1] + meridional

def smooth(fields, coeffs, count):
    padded_coeffs = jnp.pad(coeffs, ((0, 0), (1, 1), (0, 0)))
    for sweep_index in range(count):
        fields = diffuse(jnp.pad(fields, ((0, 0), (0, 0), (1, 1), (0, 0))), padded_coeffs)
    return fields

def network(profiles, w_in, b_in, w_mid, b_mid, w_out, b_out):
    shape = profiles.shape
    flat = profiles.reshape(shape[0] * shape[1], shape[2] * shape[3])
    hidden = jax.nn.gelu(jnp.dot(w_in, flat, preferred_element_type=jnp.float32) + b_in[:, None]).astype(jnp.bfloat16)
    for layer_index in range(w_mid.shape[0]):
        hidden = jax.nn.gelu(jnp.dot(w_mid[layer_index], hidden, preferred_element_type=jnp.float32) + b_mid[layer_index][:, None]).astype(jnp.bfloat16)
    output = (jnp.dot(w_out, hidden, preferred_element_type=jnp.float32) + b_out[:, None]).astype(jnp.bfloat16)
    return output.reshape(shape)

def reference(fields, region, land, coef_table, w_in, b_in, w_mid, b_mid, w_out, b_out):
    coeffs = coef_table[:, region] * (1.0 - 0.6 * land.astype(jnp.float32))[None]
    smoothed = smooth(fields, coeffs, PRE)
    profiles = smoothed.astype(jnp.bfloat16)
    blocks = profiles.reshape(V, L, N_LAT, ROWS, NLON).transpose(2, 0, 1, 3, 4)
    results = lax.map(lambda block: network(block, w_in, b_in, w_mid, b_mid, w_out, b_out), blocks)
    fluxes = results.transpose(1, 2, 0, 3, 4).reshape(V, L, N_LAT * ROWS, NLON)
    return smooth(fluxes.astype(jnp.float32), coeffs, POST)
```

```python
import functools

import jax
import jax.numpy as jnp
from jax import lax
from jax.experimental import pallas as pl
from jax.experimental.pallas import tpu as pltpu
from jax.sharding import PartitionSpec as P

PRE = 4
POST = 2
MESH = pl.DeviceIdType.MESH
BF = jnp.bfloat16
F32 = jnp.float32


def gelu(x):
    scale = 0.7978845608028654
    inner = x * (scale + (scale * 0.044715) * (x * x))
    half = 0.5 * x
    return half + half * jnp.tanh(inner)


def kernel(
    n_lat, n_var, n_lev, n_row,
    region, land, table, b_in, b_mid, b_out, fields, w_in_hbm, w_mid_hbm, w_out_hbm,
    split,
    w_in, w_mid, w_out, wi, wo,
    sent, halo, marks, f0, f1, f2, f3, ef, ew, nf, prof, other, h1, h2, flux_own, flux, bias,
    in_sem, w_sem, mark_send, mark_recv, halo_send, halo_recv, prof_send, prof_recv,
    flux_send, flux_recv, edge_send, edge_recv,
):
    lat = lax.axis_index("lat")
    lev = lax.axis_index("lev")
    peer = 1 - lev
    has_up = lat > 0
    has_down = lat < n_lat - 1
    pad_lev = ef.shape[1]
    feat = n_var * pad_lev
    n_lon = fields.shape[1]
    hid = w_mid.shape[1]
    n_mid = w_mid.shape[0]
    half = n_row // 2
    first = PRE
    last = PRE + n_row - 1

    lanes = split.shape[2]
    n_split = split.shape[0]

    def columns_of(ref, c):
        return ref.at[:, c * lanes : (c + 1) * lanes]

    pieces = [
        pltpu.make_async_copy(columns_of(fields, c), split.at[c], in_sem.at[c])
        for c in range(n_split)
    ]
    for piece in pieces:
        piece.start()
    loads = [
        pltpu.make_async_copy(w_in_hbm, w_in, w_sem.at[0]),
        pltpu.make_async_copy(w_out_hbm, w_out, w_sem.at[1]),
        pltpu.make_async_copy(w_mid_hbm, w_mid, w_sem.at[2]),
    ]
    for load in loads:
        load.start()

    barrier = pltpu.get_barrier_semaphore()
    pl.semaphore_signal(barrier, inc=1, device_id={"lev": peer}, device_id_type=MESH)

    @pl.when(has_up)
    def _():
        for j in range(2):
            pl.semaphore_signal(
                barrier, inc=1, device_id={"lat": lat - 1, "lev": j}, device_id_type=MESH
            )

    @pl.when(has_down)
    def _():
        for j in range(2):
            pl.semaphore_signal(
                barrier, inc=1, device_id={"lat": lat + 1, "lev": j}, device_id_type=MESH
            )

    def take_row(r):
        for v in range(n_var):
            base = v * n_lev * n_row
            values = jnp.concatenate(
                [split[c, pl.ds(base + r, n_lev, stride=n_row), :] for c in range(n_split)],
                axis=1,
            )
            values = jnp.concatenate(
                [values, jnp.zeros((pad_lev - n_lev, n_lon), F32)], axis=0
            )
            f0[PRE + r, v * pad_lev : (v + 1) * pad_lev, :] = values
            sent[r, v * pad_lev : (v + 1) * pad_lev, :] = values.astype(BF)

    cut = feat // 2

    def row_up(k, h):
        part = pl.ds(h * cut, cut)
        return pltpu.make_async_remote_copy(
            src_ref=sent.at[k, part], dst_ref=halo.at[1, k, part],
            send_sem=halo_send.at[1, k, h], recv_sem=halo_recv.at[1, k, h],
            device_id={"lat": lat - 1}, device_id_type=MESH,
        )

    def row_down(k, h):
        part = pl.ds(h * cut, cut)
        return pltpu.make_async_remote_copy(
            src_ref=sent.at[n_row - 1 - k, part], dst_ref=halo.at[0, k, part],
            send_sem=halo_send.at[0, k, h], recv_sem=halo_recv.at[0, k, h],
            device_id={"lat": lat + 1}, device_id_type=MESH,
        )

    def marks_to(side, which, source, target):
        return pltpu.make_async_remote_copy(
            src_ref=source, dst_ref=marks.at[side, which],
            send_sem=mark_send.at[side, which], recv_sem=mark_recv.at[side, which],
            device_id={"lat": target}, device_id_type=MESH,
        )

    for piece in pieces:
        piece.wait()
    take_row(0)
    take_row(n_row - 1)

    pl.semaphore_wait(barrier, 1 + 2 * has_up.astype(jnp.int32) + 2 * has_down.astype(jnp.int32))

    @pl.when(has_up)
    def _():
        marks_to(1, 0, region, lat - 1).start()
        marks_to(1, 1, land, lat - 1).start()
        row_up(0, 0).start()
        row_up(0, 1).start()

    @pl.when(has_down)
    def _():
        marks_to(0, 0, region, lat + 1).start()
        marks_to(0, 1, land, lat + 1).start()
        row_down(0, 0).start()
        row_down(0, 1).start()

    for k in range(1, PRE):
        take_row(k)
        take_row(n_row - 1 - k)
        if k == 1:

            @pl.when(has_up)
            def _():
                row_up(1, 0).start()

            @pl.when(has_down)
            def _():
                row_down(1, 0).start()

    n_region, all_lev = table.shape
    wide = jnp.concatenate([table[...], jnp.zeros((n_region, 128 - all_lev), F32)], axis=1)
    wide = pltpu.roll(wide, (128 - lev * n_lev) % 128, 1)
    wide = jnp.concatenate([wide] * (128 // n_region), axis=0).T[:pad_lev]
    level_id = lax.broadcasted_iota(jnp.int32, (pad_lev, 128), 0)
    wide = jnp.where(level_id < n_lev, wide, 0.0)
    columns = [
        jnp.broadcast_to(wide[:, k : k + 1], (pad_lev, n_lon)) for k in range(n_region)
    ]

    def coefficient(region_row, land_row):
        region_row = jnp.broadcast_to(region_row, (pad_lev, n_lon))
        total = columns[0]
        for k in range(1, len(columns)):
            total = jnp.where(region_row == k, columns[k], total)
        return total * (1.0 - 0.6 * land_row.astype(F32))

    for r in range(n_row):
        ef[first + r] = coefficient(region[r : r + 1, :], land[r : r + 1, :])

    def faces_north(i):
        nf[i] = jnp.sqrt(ef[i] * ef[i + 1])

    def faces_east(i):
        c = ef[i]
        east = jnp.sqrt(c * pltpu.roll(c, n_lon - 1, 1))
        ef[i] = east
        ew[i] = pltpu.roll(east, 1, 1)

    for i in range(first, last):
        faces_north(i)

    def step_rows(src, dst, i, store=None):
        size = 8 if store is None else 16
        for s in range(0, pad_lev, size):
            east = ef[i, s : s + size, :]
            west = ew[i, s : s + size, :]
            north = nf[i, s : s + size, :]
            south = nf[i - 1, s : s + size, :]
            for v in range(n_var):
                rows = slice(v * pad_lev + s, v * pad_lev + s + size)
                f = src[i, rows, :]
                zonal = east * (pltpu.roll(f, n_lon - 1, 1) - f) - west * (
                    f - pltpu.roll(f, 1, 1)
                )
                meridional = north * (src[i + 1, rows, :] - f) - south * (
                    f - src[i - 1, rows, :]
                )
                value = f + zonal + meridional
                if store is None:
                    dst[i, rows, :] = value
                else:
                    store(v, s, rows, value)

    def loop_rows(low, high, fn):
        def body(i, carry):
            fn(i)
            return carry

        lax.fori_loop(low, high, body, 0)

    for side in range(2):
        exists = has_up if side == 0 else has_down

        @pl.when(exists)
        def _():
            for which in range(2):
                marks_to(side, which, region, lat).wait_recv()
            for k in range(PRE):
                r = n_row - 1 - k if side == 0 else k
                i = first - 1 - k if side == 0 else last + 1 + k
                ef[i] = coefficient(
                    marks[side, 0, r : r + 1, :], marks[side, 1, r : r + 1, :]
                )

        @pl.when(jnp.logical_not(exists))
        def _():
            for k in range(PRE):
                i = first - 1 - k if side == 0 else last + 1 + k
                ef[i] = jnp.zeros((pad_lev, n_lon), F32)
                f0[i] = jnp.zeros((feat, n_lon), F32)

    for i in list(range(0, first)) + list(range(last, last + PRE)):
        faces_north(i)
    for i in range(0, last + PRE + 1):
        faces_east(i)

    loop_rows(first + 1, last, lambda i: step_rows(f0, f1, i))
    loop_rows(first + 2, last - 1, lambda i: step_rows(f1, f2, i))
    loop_rows(first + 3, last - 2, lambda i: step_rows(f2, f3, i))

    loads[0].wait()
    loads[1].wait()
    n_feat = w_out.shape[0]
    for j in range(2):
        f_id = lax.broadcasted_iota(jnp.int32, (feat, n_feat), 1)
        c_id = lax.broadcasted_iota(jnp.int32, (feat, n_feat), 0)
        l_id = c_id % pad_lev
        want = (c_id // pad_lev) * (2 * n_lev) + j * n_lev + l_id
        pick = jnp.where((f_id == want) & (l_id < n_lev), 1.0, 0.0).astype(BF)
        wi[j] = jnp.dot(pick, w_in[...], preferred_element_type=F32).T.astype(BF)
        wo[j] = jnp.dot(pick, w_out[...], preferred_element_type=F32).astype(BF)

    def tall(row):
        return jnp.broadcast_to(row, (128, 128)).T

    start = (n_mid + 1) * hid
    for m in range(0, n_feat, 128):
        count = min(128, n_feat - m)
        row = b_out[m : m + count].reshape(1, count)
        if count < 128:
            row = jnp.concatenate([row, jnp.zeros((1, 128 - count), F32)], axis=1)
        bias[m : m + 128, :] = tall(row)
    bias[start : start + 2 * feat, :] = jnp.zeros((2 * feat, 128), F32)
    for v in range(n_var):
        for j in range(2):
            place = start + j * feat + v * pad_lev
            origin = v * 2 * n_lev + j * n_lev
            bias[place : place + n_lev, :] = bias[origin : origin + n_lev, :]
    for m in range(0, hid, 128):
        bias[m : m + 128, :] = tall(b_in[:, m : m + 128])
        for layer in range(n_mid):
            start = (layer + 1) * hid + m
            bias[start : start + 128, :] = tall(b_mid[layer : layer + 1, m : m + 128])
    loads[2].wait()

    tile = 256

    def with_bias(x, start, size):
        b = bias[start : start + size, :]
        return x + jnp.concatenate([b] * (n_lon // b.shape[1]), axis=1)

    def profile_copy(p):
        return pltpu.make_async_remote_copy(
            src_ref=prof.at[peer, p], dst_ref=other.at[p],
            send_sem=prof_send.at[p], recv_sem=prof_recv.at[p],
            device_id={"lev": peer}, device_id_type=MESH,
        )

    def flux_row(owner, p):
        return half - 1 - p + owner * (1 + 2 * p)

    def flux_copy(p):
        return pltpu.make_async_remote_copy(
            src_ref=flux_own.at[p, peer], dst_ref=flux.at[flux_row(lev, p) + POST],
            send_sem=flux_send.at[p], recv_sem=flux_recv.at[p],
            device_id={"lev": peer}, device_id_type=MESH,
        )

    def edge_copy(p, j):
        q = p - (half - POST)
        place = flux_row(lev, p) + POST + (1 - 2 * lev) * n_row
        return pltpu.make_async_remote_copy(
            src_ref=flux_own.at[p, j], dst_ref=flux.at[place],
            send_sem=edge_send.at[q, j], recv_sem=edge_recv.at[peer, q],
            device_id={"lat": lat - 1 + 2 * lev, "lev": j}, device_id_type=MESH,
        )

    has_edge = jnp.where(lev == 0, has_up, has_down)

    def phase(p, carry):
        for side in range(2):
            exists = has_up if side == 0 else has_down

            @pl.when(exists)
            def _():
                if side == 0:
                    row_down(p, 0).wait_recv()
                    row_down(p, 1).wait_recv()
                    f0[first - 1 - p] = halo[0, p].astype(F32)
                else:
                    row_up(p, 0).wait_recv()
                    row_up(p, 1).wait_recv()
                    f0[last + 1 + p] = halo[1, p].astype(F32)

        def save(side):
            def store(v, s, rows, value):
                prof[side, p, rows, :] = value.astype(BF)

            return store

        for k, (src, dst) in enumerate(((f0, f1), (f1, f2), (f2, f3), (f3, None))):
            for side in range(2):
                at = first - p + k if side == 0 else last + p - k
                step_rows(src, dst, at, save(side) if dst is None else None)
        exchange = profile_copy(p)
        exchange.start()

        for exists, row in ((has_up, row_up), (has_down, row_down)):

            @pl.when(exists & (p < PRE - 1))
            def _():
                row(p + 1, 1).start()

            @pl.when(exists & (p < PRE - 2))
            def _():
                row(p + 2, 0).start()

        @pl.when(has_edge & (p > half - POST))
        def _():
            edge_copy(p - 1, 1).start()

        exchange.wait_recv()

        for m in range(0, hid, tile):
            x = jnp.dot(wi[lev, m : m + tile, :], prof[lev, p], preferred_element_type=F32)
            x = x + jnp.dot(
                wi[peer, m : m + tile, :], other[p], preferred_element_type=F32
            )
            h1[m : m + tile, :] = gelu(with_bias(x, m, tile)).astype(BF)
        now, then = h1, h2
        for layer in range(n_mid):
            for m in range(0, hid, tile):
                x = jnp.dot(w_mid[layer, m : m + tile, :], now[...], preferred_element_type=F32)
                x = with_bias(x, (layer + 1) * hid + m, tile)
                then[m : m + tile, :] = gelu(x).astype(BF)
            now, then = then, now
        for j in range(2):
            x = jnp.dot(wo[j], now[...], preferred_element_type=F32)
            flux_own[p, j] = with_bias(x, (n_mid + 1) * hid + j * feat, feat).astype(BF)
        flux[flux_row(lev, p) + POST] = flux_own[p, lev]
        flux_copy(p).start()

        @pl.when(has_edge & (p >= half - POST))
        def _():
            edge_copy(p, 0).start()

        return carry

    lax.fori_loop(0, PRE, phase, 0)

    @pl.when(has_edge)
    def _():
        edge_copy(half - 1, 1).start()

    for p in range(half):
        flux_copy(p).wait_recv()

    def widen(i):
        f0[i] = flux[i - PRE + POST].astype(F32)

    loop_rows(first, last + 1, widen)

    def finish(i):
        def store(v, s, rows, value):
            count = min(16, n_lev - s)
            base = v * (n_lev * n_row) + s * n_row + (i - first)
            for c in range(n_split):
                split[c, pl.ds(base, count, stride=n_row), :] = value[
                    :count, c * lanes : (c + 1) * lanes
                ]

        step_rows(f1, None, i, store)

    loop_rows(first + 1, last, lambda i: step_rows(f0, f1, i))
    loop_rows(first + 2, last - 1, finish)

    for side in range(2):
        exists = has_up if side == 0 else has_down

        @pl.when(exists)
        def _():
            for q in range(POST):
                pltpu.make_async_remote_copy(
                    src_ref=flux_own.at[0, 0], dst_ref=flux.at[0],
                    send_sem=edge_send.at[0, 0], recv_sem=edge_recv.at[side, q],
                    device_id={"lev": peer}, device_id_type=MESH,
                ).wait_recv()
            for q in range(POST):
                widen(first - 1 - q if side == 0 else last + 1 + q)

    for i in (first - 1, first, last, last + 1):
        step_rows(f0, f1, i)
    for i in (first, first + 1, last - 1, last):
        finish(i)
    for k in range(PRE):
        profile_copy(k).wait_send()
        flux_copy(k).wait_send()

    @pl.when(has_up)
    def _():
        for which in range(2):
            marks_to(1, which, region, lat).wait_send()
        for k in range(PRE):
            row_up(k, 0).wait_send()
            row_up(k, 1).wait_send()

    @pl.when(has_down)
    def _():
        for which in range(2):
            marks_to(0, which, region, lat).wait_send()
        for k in range(PRE):
            row_down(k, 0).wait_send()
            row_down(k, 1).wait_send()

    @pl.when(has_edge)
    def _():
        for p in range(half - POST, half):
            for j in range(2):
                edge_copy(p, j).wait_send()


def write_out(split, out, sem):
    lanes = split.shape[2]
    pieces = [
        pltpu.make_async_copy(split.at[c], out.at[:, c * lanes : (c + 1) * lanes], sem.at[c])
        for c in range(split.shape[0])
    ]
    for piece in pieces:
        piece.start()
    for piece in pieces:
        piece.wait()


def per_device(n_lat, fields, region, land, coef_table, w_in, b_in, w_mid, b_mid, w_out, b_out):
    n_var, n_lev, n_row, n_lon = fields.shape
    hid = w_in.shape[0]
    pad_lev = -(-n_lev // 16) * 16
    feat = n_var * pad_lev
    rows = n_row + 2 * PRE
    n_split = n_lon // 128
    n_all = n_var * n_lev * n_row
    dma = pltpu.SemaphoreType.DMA
    vmem = pl.BlockSpec(memory_space=pltpu.VMEM)
    hbm = pl.BlockSpec(memory_space=pl.ANY)
    result = pl.pallas_call(
        functools.partial(kernel, n_lat, n_var, n_lev, n_row),
        out_shape=pltpu.VMEM((n_split, n_all, 128), F32),
        in_specs=[vmem] * 6 + [hbm] * 4,
        out_specs=vmem,
        scratch_shapes=[
            pltpu.VMEM(w_in.shape[::-1], BF),
            pltpu.VMEM(w_mid.shape, BF),
            pltpu.VMEM(w_out.shape, BF),
            pltpu.VMEM((2, hid, feat), BF),
            pltpu.VMEM((2, feat, hid), BF),
            pltpu.VMEM((n_row, feat, n_lon), BF),
            pltpu.VMEM((2, PRE, feat, n_lon), BF),
            pltpu.VMEM((2, 2, n_row, n_lon), jnp.int32),
            pltpu.VMEM((rows, feat, n_lon), F32),
            pltpu.VMEM((rows, feat, n_lon), F32),
            pltpu.VMEM((rows, feat, n_lon), F32),
            pltpu.VMEM((rows, feat, n_lon), F32),
            pltpu.VMEM((rows, pad_lev, n_lon), F32),
            pltpu.VMEM((rows, pad_lev, n_lon), F32),
            pltpu.VMEM((rows, pad_lev, n_lon), F32),
            pltpu.VMEM((2, PRE, feat, n_lon), BF),
            pltpu.VMEM((PRE, feat, n_lon), BF),
            pltpu.VMEM((hid, n_lon), BF),
            pltpu.VMEM((hid, n_lon), BF),
            pltpu.VMEM((PRE, 2, feat, n_lon), BF),
            pltpu.VMEM((n_row + 2 * POST, feat, n_lon), BF),
            pltpu.VMEM(((w_mid.shape[0] + 1) * hid + 2 * feat, 128), F32),
            dma((n_split,)),
            dma((3,)),
            dma((2, 2)),
            dma((2, 2)),
            dma((2, PRE, 2)),
            dma((2, PRE, 2)),
            dma((PRE,)),
            dma((PRE,)),
            dma((PRE,)),
            dma((PRE,)),
            dma((POST, 2)),
            dma((2, POST)),
        ],
        compiler_params=pltpu.CompilerParams(
            collective_id=0, has_side_effects=True, vmem_limit_bytes=60 * 2**20
        ),
    )(
        region, land, coef_table.T, b_in.reshape(1, -1), b_mid, b_out,
        fields.reshape(n_all, n_lon), w_in.T, w_mid, w_out,
    )
    closure = pl.pallas_call(
        write_out,
        out_shape=jax.ShapeDtypeStruct((n_all, n_lon), F32),
        in_specs=[vmem],
        out_specs=hbm,
        scratch_shapes=[dma((n_split,))],
    )(pltpu.with_memory_space_constraint(result, pltpu.VMEM))
    return closure.reshape(fields.shape)


def solution(mesh):
    placed = (
        P(None, "lev", ("parts", "lat"), None),
        P(("parts", "lat"), None),
        P(("parts", "lat"), None),
    ) + (P(),) * 7
    return jax.shard_map(
        functools.partial(per_device, mesh.shape["lat"]),
        mesh=mesh,
        in_specs=placed,
        out_specs=P(None, "lev", ("parts", "lat"), None),
        check_vma=False,
    )
```

```python
import functools

import jax
import jax.numpy as jnp
from jax import lax
from jax.experimental import pallas as pl
from jax.experimental.pallas import tpu as pltpu
from jax.sharding import PartitionSpec as P

PRE = 4
POST = 2
MESH = pl.DeviceIdType.MESH
BF = jnp.bfloat16
F32 = jnp.float32


SCALE = 0.7978845608028654


def gelu(x):
    inner = x * (SCALE + (SCALE * 0.044715) * (x * x))
    half = 0.5 * x
    return half + half * jnp.tanh(inner)


def gelu_of_half(half):
    inner = half * (2.0 * SCALE + (8.0 * SCALE * 0.044715) * (half * half))
    return half + half * jnp.tanh(inner)


def kernel(
    n_lat, folded, n_var, n_lev, n_row,
    region_hbm, land_hbm, table_hbm, b_in_hbm, b_mid_hbm, b_out_hbm,
    fields, w_in_hbm, w_mid_hbm, w_out_hbm,
    split,
    region, land, table, b_in, b_mid, b_out, w_in, w_mid, w_out, wi, wo,
    sent, halo, passed, marks, f0, f1, f2, f3, ef, ew, nf, cf, prof, cols, h1, h2, flux_own, flux, bias,
    in_sem, small_sem, w_sem, mark_send, mark_recv, halo_send, halo_recv, passed_send, passed_recv, prof_send, prof_recv,
    flux_send, flux_recv, edge_send, edge_recv,
):
    lat = lax.axis_index("lat")
    lev = lax.axis_index("lev")
    peer = 1 - lev
    has_up = lat > 0
    has_down = lat < n_lat - 1
    odd = lat % 2
    pair = lat // 2
    n_pair = n_lat // 2
    above = pair * PRE // n_pair
    below = (n_pair - 1 - pair) * PRE // n_pair
    first_mine = PRE - jnp.where(odd == 1, below, above)
    first_passed = PRE - jnp.where(odd == 1, above, below)
    target = lat + 2 - 4 * odd
    source = lat - 2 + 4 * odd
    has_target = (target >= 0) & (target < n_lat)
    has_source = (source >= 0) & (source < n_lat)
    pad_lev = ef.shape[1]
    feat = n_var * pad_lev
    n_lon = fields.shape[1]
    hid = w_mid.shape[1]
    n_mid = w_mid.shape[0]
    half = n_row // 2
    first = PRE
    last = PRE + n_row - 1

    lanes = split.shape[2]
    n_split = split.shape[0]

    barrier = pltpu.get_barrier_semaphore()
    pl.semaphore_signal(barrier, inc=1, device_id={"lev": peer}, device_id_type=MESH)

    @pl.when(has_up)
    def _():
        for j in range(2):
            pl.semaphore_signal(
                barrier, inc=1, device_id={"lat": lat - 1, "lev": j}, device_id_type=MESH
            )

    @pl.when(has_down)
    def _():
        for j in range(2):
            pl.semaphore_signal(
                barrier, inc=1, device_id={"lat": lat + 1, "lev": j}, device_id_type=MESH
            )

    if folded:

        @pl.when(has_source)
        def _():
            pl.semaphore_signal(barrier, inc=1, device_id={"lat": source}, device_id_type=MESH)

    def columns_of(ref, c):
        return ref.at[:, c * lanes : (c + 1) * lanes]

    pieces = [
        pltpu.make_async_copy(columns_of(fields, c), split.at[c], in_sem.at[c])
        for c in range(n_split)
    ]
    for piece in pieces:
        piece.start()
    small = [
        pltpu.make_async_copy(source, target, small_sem.at[k])
        for k, (source, target) in enumerate((
            (region_hbm, region), (land_hbm, land), (table_hbm, table),
            (b_in_hbm, b_in), (b_mid_hbm, b_mid), (b_out_hbm, b_out),
        ))
    ]
    for piece in small:
        piece.start()
    loads = [
        pltpu.make_async_copy(w_in_hbm, w_in, w_sem.at[0]),
        pltpu.make_async_copy(w_out_hbm, w_out, w_sem.at[1]),
        pltpu.make_async_copy(w_mid_hbm, w_mid, w_sem.at[2]),
    ]

    def take_row(r):
        for v in range(n_var):
            base = v * n_lev * n_row
            values = jnp.concatenate(
                [split[c, pl.ds(base + r, n_lev, stride=n_row), :] for c in range(n_split)],
                axis=1,
            )
            values = jnp.concatenate(
                [values, jnp.ones((pad_lev - n_lev, n_lon), F32)], axis=0
            )
            f0[PRE + r, v * pad_lev : (v + 1) * pad_lev, :] = values
            sent[r, v * pad_lev : (v + 1) * pad_lev, :] = values.astype(BF)

    cut = feat // 2

    def row_up(k, h):
        part = pl.ds(h * cut, cut)
        return pltpu.make_async_remote_copy(
            src_ref=sent.at[k, part], dst_ref=halo.at[1, k, part],
            send_sem=halo_send.at[1, k, h], recv_sem=halo_recv.at[1, k, h],
            device_id={"lat": lat - 1}, device_id_type=MESH,
        )

    def row_down(k, h):
        part = pl.ds(h * cut, cut)
        return pltpu.make_async_remote_copy(
            src_ref=sent.at[n_row - 1 - k, part], dst_ref=halo.at[0, k, part],
            send_sem=halo_send.at[0, k, h], recv_sem=halo_recv.at[0, k, h],
            device_id={"lat": lat + 1}, device_id_type=MESH,
        )

    def by_pair(side, k):
        return (odd == 1 - side) & (k >= first_mine) if folded else lat < 0

    def to_pair(side, k, h):
        part = pl.ds(h * cut, cut)
        row = n_row - 1 - k if side == 0 else k
        return pltpu.make_async_remote_copy(
            src_ref=sent.at[row, part], dst_ref=passed.at[k - 1, part],
            send_sem=halo_send.at[side, k, h], recv_sem=passed_recv.at[k - 1, h],
            device_id={"lat": lat + 1 - 2 * odd}, device_id_type=MESH,
        )

    def pass_on(k, h):
        part = pl.ds(h * cut, cut)
        return pltpu.make_async_remote_copy(
            src_ref=passed.at[k - 1, part], dst_ref=halo.at[odd, k, part],
            send_sem=passed_send.at[k - 1, h], recv_sem=halo_recv.at[odd, k, h],
            device_id={"lat": target}, device_id_type=MESH,
        )

    def send_row(side, k, h):
        exists, row = ((has_down, row_down), (has_up, row_up))[side]

        @pl.when(exists & jnp.logical_not(by_pair(side, k)))
        def _():
            row(k, h).start()

    def send_pair(side, k):
        if folded:
            exists = (has_down, has_up)[side]

            @pl.when(exists & by_pair(side, k))
            def _():
                to_pair(side, k, 0).start()
                to_pair(side, k, 1).start()

    def marks_to(side, which, source, target):
        return pltpu.make_async_remote_copy(
            src_ref=source, dst_ref=marks.at[side, which],
            send_sem=mark_send.at[side, which], recv_sem=mark_recv.at[side, which],
            device_id={"lat": target}, device_id_type=MESH,
        )

    for piece in pieces + small:
        piece.wait()
    take_row(0)
    take_row(n_row - 1)
    for load in loads:
        load.start()

    greeted = 1 + 2 * has_up.astype(jnp.int32) + 2 * has_down.astype(jnp.int32)
    if folded:
        greeted = greeted + has_target.astype(jnp.int32)
    pl.semaphore_wait(barrier, greeted)

    @pl.when(has_up)
    def _():
        marks_to(1, 0, region, lat - 1).start()
        marks_to(1, 1, land, lat - 1).start()
        row_up(0, 0).start()
        row_up(0, 1).start()

    @pl.when(has_down)
    def _():
        marks_to(0, 0, region, lat + 1).start()
        marks_to(0, 1, land, lat + 1).start()
        row_down(0, 0).start()
        row_down(0, 1).start()

    for k in range(1, PRE):
        take_row(k)
        take_row(n_row - 1 - k)
        if k == 1:
            send_pair(1, 1)
            send_pair(0, 1)

    n_region, all_lev = table.shape
    wide = jnp.concatenate([table[...], jnp.zeros((n_region, 128 - all_lev), F32)], axis=1)
    wide = pltpu.roll(wide, (128 - lev * n_lev) % 128, 1)
    wide = jnp.concatenate([wide] * (128 // n_region), axis=0).T[:pad_lev]
    level_id = lax.broadcasted_iota(jnp.int32, (pad_lev, 128), 0)
    wide = jnp.where(level_id < n_lev, wide, 0.0)
    columns = [
        jnp.broadcast_to(wide[:, k : k + 1], (pad_lev, n_lon)) for k in range(n_region)
    ]

    def coefficient(region_row, land_row):
        region_row = jnp.broadcast_to(region_row, (pad_lev, n_lon))
        total = columns[0]
        for k in range(1, len(columns)):
            total = jnp.where(region_row == k, columns[k], total)
        return total * (1.0 - 0.6 * land_row.astype(F32))

    for r in range(n_row):
        ef[first + r] = coefficient(region[r : r + 1, :], land[r : r + 1, :])

    def faces_north(i):
        nf[i] = jnp.sqrt(ef[i] * ef[i + 1])

    def faces_east(i):
        c = ef[i]
        east = jnp.sqrt(c * pltpu.roll(c, n_lon - 1, 1))
        ef[i] = east
        ew[i] = pltpu.roll(east, 1, 1)

    for i in range(first, last):
        faces_north(i)

    def centre(i):
        cf[i] = 1.0 - ((ef[i] + ew[i]) + (nf[i] + nf[i - 1]))

    def step_rows(src, dst, i, store=None):
        size = 8 if store is None else 16
        for s in range(0, pad_lev, size):
            own = cf[i, s : s + size, :]
            east = ef[i, s : s + size, :]
            west = ew[i, s : s + size, :]
            north = nf[i, s : s + size, :]
            south = nf[i - 1, s : s + size, :]
            for v in range(n_var):
                rows = slice(v * pad_lev + s, v * pad_lev + s + size)
                f = src[i, rows, :]
                zonal = east * pltpu.roll(f, n_lon - 1, 1) + west * pltpu.roll(f, 1, 1)
                meridional = north * src[i + 1, rows, :] + south * src[i - 1, rows, :]
                value = (own * f + zonal) + meridional
                if store is None:
                    dst[i, rows, :] = value
                else:
                    store(v, s, rows, value)

    def loop_rows(low, high, fn):
        def body(i, carry):
            fn(i)
            return carry

        lax.fori_loop(low, high, body, 0)

    for side in range(2):
        exists = has_up if side == 0 else has_down

        @pl.when(exists)
        def _():
            for which in range(2):
                marks_to(side, which, region, lat).wait_recv()
            for k in range(PRE):
                r = n_row - 1 - k if side == 0 else k
                i = first - 1 - k if side == 0 else last + 1 + k
                ef[i] = coefficient(
                    marks[side, 0, r : r + 1, :], marks[side, 1, r : r + 1, :]
                )

        @pl.when(jnp.logical_not(exists))
        def _():
            for k in range(PRE):
                i = first - 1 - k if side == 0 else last + 1 + k
                ef[i] = jnp.zeros((pad_lev, n_lon), F32)
                f0[i] = jnp.zeros((feat, n_lon), F32)

    for i in list(range(0, first)) + list(range(last, last + PRE)):
        faces_north(i)
    for i in range(0, last + PRE + 1):
        faces_east(i)
    for i in range(1, last + PRE):
        centre(i)

    send_row(1, 1, 0)
    send_row(0, 1, 0)

    loop_rows(first + 1, last, lambda i: step_rows(f0, f1, i))
    loop_rows(first + 2, last - 1, lambda i: step_rows(f1, f2, i))
    loop_rows(first + 3, last - 2, lambda i: step_rows(f2, f3, i))

    loads[0].wait()
    loads[1].wait()
    n_feat = w_out.shape[0]
    f_id = lax.broadcasted_iota(jnp.int32, (feat, n_feat), 1)
    c_id = lax.broadcasted_iota(jnp.int32, (feat, n_feat), 0)
    l_id = c_id % pad_lev
    half_b = 0.5 * b_in[...]
    b_parts = []
    for _ in range(3):
        b_parts.append(half_b.astype(BF))
        half_b = half_b - b_parts[-1].astype(F32)
    place_id = lax.broadcasted_iota(jnp.int32, (feat, hid), 0)
    for j in range(2):
        want = (c_id // pad_lev) * (2 * n_lev) + j * n_lev + l_id
        found = (f_id == want) & (l_id < n_lev)
        halves = jnp.where(found, 0.5, 0.0).astype(BF)
        weight = jnp.dot(halves, w_in[...], preferred_element_type=F32)
        if j == 0:
            for place, part in zip((n_lev, n_lev + 1, pad_lev + n_lev), b_parts):
                weight = jnp.where(place_id == place, part.astype(F32), weight)
        wi[:, j * feat : (j + 1) * feat] = weight.T.astype(BF)
        pick = jnp.where(found, 1.0, 0.0).astype(BF)
        wo[j] = jnp.dot(pick, w_out[...], preferred_element_type=F32).astype(BF)

    def tall(row):
        return jnp.broadcast_to(row, (128, 128)).T

    start = n_mid * hid
    for m in range(0, n_feat, 128):
        count = min(128, n_feat - m)
        row = b_out[m : m + count].reshape(1, count)
        if count < 128:
            row = jnp.concatenate([row, jnp.zeros((1, 128 - count), F32)], axis=1)
        bias[m : m + 128, :] = tall(row)
    bias[start : start + 2 * feat, :] = jnp.zeros((2 * feat, 128), F32)
    for v in range(n_var):
        for j in range(2):
            place = start + j * feat + v * pad_lev
            origin = v * 2 * n_lev + j * n_lev
            bias[place : place + n_lev, :] = bias[origin : origin + n_lev, :]
    for m in range(0, hid, 128):
        for layer in range(n_mid):
            start = layer * hid + m
            bias[start : start + 128, :] = tall(b_mid[layer : layer + 1, m : m + 128])
    loads[2].wait()

    tile = 256

    def with_bias(x, start, size):
        b = bias[start : start + size, :]
        return x + jnp.concatenate([b] * (n_lon // b.shape[1]), axis=1)

    def profile_copy(p):
        return pltpu.make_async_remote_copy(
            src_ref=prof.at[p], dst_ref=cols.at[p, pl.ds(lev * feat, feat)],
            send_sem=prof_send.at[p], recv_sem=prof_recv.at[p],
            device_id={"lev": peer}, device_id_type=MESH,
        )

    def flux_row(owner, p):
        return half - 1 - p + owner * (1 + 2 * p)

    def flux_copy(p):
        return pltpu.make_async_remote_copy(
            src_ref=flux_own.at[p, peer], dst_ref=flux.at[flux_row(lev, p) + POST],
            send_sem=flux_send.at[p], recv_sem=flux_recv.at[p],
            device_id={"lev": peer}, device_id_type=MESH,
        )

    def edge_copy(p, j):
        q = p - (half - POST)
        place = flux_row(lev, p) + POST + (1 - 2 * lev) * n_row
        return pltpu.make_async_remote_copy(
            src_ref=flux_own.at[p, j], dst_ref=flux.at[place],
            send_sem=edge_send.at[q, j], recv_sem=edge_recv.at[peer, q],
            device_id={"lat": lat - 1 + 2 * lev, "lev": j}, device_id_type=MESH,
        )

    has_edge = jnp.where(lev == 0, has_up, has_down)

    def smooth(p, side, store):
        @pl.when(jnp.where(side == 0, has_up, has_down))
        def _():
            for h in range(2):
                part = pl.ds(h * cut, cut)
                pltpu.make_async_remote_copy(
                    src_ref=sent.at[0, part], dst_ref=halo.at[side, p, part],
                    send_sem=halo_send.at[side, p, h], recv_sem=halo_recv.at[side, p, h],
                    device_id={"lev": peer}, device_id_type=MESH,
                ).wait_recv()
            f0[jnp.where(side == 0, first - 1 - p, last + 1 + p)] = halo[side, p].astype(F32)

        for k, (src, dst) in enumerate(((f0, f1), (f1, f2), (f2, f3), (f3, None))):
            at = jnp.where(side == 0, first - p + k, last + p - k)
            step_rows(src, dst, at, store if dst is None else None)

    def phase(p, carry):
        def save_peer(v, s, rows, value):
            prof[p, rows, :] = value.astype(BF)

        def save_own(v, s, rows, value):
            place = pl.multiple_of(lev * feat + rows.start, 16)
            cols[p, pl.ds(place, rows.stop - rows.start), :] = value.astype(BF)

        smooth(p, peer, save_peer)
        exchange = profile_copy(p)
        exchange.start()
        smooth(p, lev, save_own)

        @pl.when(p < PRE - 1)
        def _():
            for side in (1, 0):
                send_row(side, p + 1, 1)

        @pl.when(p < PRE - 2)
        def _():
            for side in (1, 0):
                send_pair(side, p + 2)

        @pl.when(has_edge & (p > half - POST))
        def _():
            edge_copy(p - 1, 1).start()

        if folded:

            @pl.when(has_target & (p < PRE - 1) & (p + 1 >= first_passed))
            def _():
                for h in range(2):
                    to_pair(0, p + 1, h).wait_recv()
                    pass_on(p + 1, h).start()

        pltpu.make_async_remote_copy(
            src_ref=prof.at[p], dst_ref=cols.at[p, pl.ds(peer * feat, feat)],
            send_sem=prof_send.at[p], recv_sem=prof_recv.at[p],
            device_id={"lev": peer}, device_id_type=MESH,
        ).wait_recv()

        for m in range(0, hid, tile):
            x = jnp.dot(wi[m : m + tile, :], cols[p], preferred_element_type=F32)
            h1[m : m + tile, :] = gelu_of_half(x).astype(BF)
        now, then = h1, h2
        for layer in range(n_mid):
            for m in range(0, hid, tile):
                x = jnp.dot(w_mid[layer, m : m + tile, :], now[...], preferred_element_type=F32)
                x = with_bias(x, layer * hid + m, tile)
                then[m : m + tile, :] = gelu(x).astype(BF)
            now, then = then, now
        for j in range(2):
            x = jnp.dot(wo[j], now[...], preferred_element_type=F32)
            flux_own[p, j] = with_bias(x, n_mid * hid + j * feat, feat).astype(BF)
        @pl.when(p < PRE - 2)
        def _():
            for side in (1, 0):
                send_row(side, p + 2, 0)

        flux[flux_row(lev, p) + POST] = flux_own[p, lev]
        flux_copy(p).start()

        @pl.when(has_edge & (p >= half - POST))
        def _():
            edge_copy(p, 0).start()

        return carry

    lax.fori_loop(0, PRE, phase, 0)

    @pl.when(has_edge)
    def _():
        edge_copy(half - 1, 1).start()

    for p in range(half):
        flux_copy(p).wait_recv()

    def widen(i):
        f0[i] = flux[i - PRE + POST].astype(F32)

    loop_rows(first, last + 1, widen)

    def finish(i):
        def store(v, s, rows, value):
            count = min(16, n_lev - s)
            base = v * (n_lev * n_row) + s * n_row + (i - first)
            for c in range(n_split):
                split[c, pl.ds(base, count, stride=n_row), :] = value[
                    :count, c * lanes : (c + 1) * lanes
                ]

        step_rows(f1, None, i, store)

    loop_rows(first + 1, last, lambda i: step_rows(f0, f1, i))
    loop_rows(first + 2, last - 1, finish)

    for side in range(2):
        exists = has_up if side == 0 else has_down

        @pl.when(exists)
        def _():
            for q in range(POST):
                pltpu.make_async_remote_copy(
                    src_ref=flux_own.at[0, 0], dst_ref=flux.at[0],
                    send_sem=edge_send.at[0, 0], recv_sem=edge_recv.at[side, q],
                    device_id={"lev": peer}, device_id_type=MESH,
                ).wait_recv()
            for q in range(POST):
                widen(first - 1 - q if side == 0 else last + 1 + q)

    for i in (first - 1, first, last, last + 1):
        step_rows(f0, f1, i)
    for i in (first, first + 1, last - 1, last):
        finish(i)
    for k in range(PRE):
        profile_copy(k).wait_send()
        flux_copy(k).wait_send()

    @pl.when(has_up)
    def _():
        for which in range(2):
            marks_to(1, which, region, lat).wait_send()
        for k in range(PRE):
            row_up(k, 0).wait_send()
            row_up(k, 1).wait_send()

    @pl.when(has_down)
    def _():
        for which in range(2):
            marks_to(0, which, region, lat).wait_send()
        for k in range(PRE):
            row_down(k, 0).wait_send()
            row_down(k, 1).wait_send()

    if folded:
        for k in range(1, PRE):

            @pl.when(has_target & (k >= first_passed))
            def _():
                for h in range(2):
                    pass_on(k, h).wait_send()

    @pl.when(has_edge)
    def _():
        for p in range(half - POST, half):
            for j in range(2):
                edge_copy(p, j).wait_send()


def write_out(split, out, sem):
    lanes = split.shape[2]
    pieces = [
        pltpu.make_async_copy(split.at[c], out.at[:, c * lanes : (c + 1) * lanes], sem.at[c])
        for c in range(split.shape[0])
    ]
    for piece in pieces:
        piece.start()
    for piece in pieces:
        piece.wait()


def per_device(n_lat, fields, region, land, coef_table, w_in, b_in, w_mid, b_mid, w_out, b_out):
    n_var, n_lev, n_row, n_lon = fields.shape
    hid = w_in.shape[0]
    pad_lev = -(-n_lev // 16) * 16
    feat = n_var * pad_lev
    rows = n_row + 2 * PRE
    n_split = n_lon // 128
    n_all = n_var * n_lev * n_row
    dma = pltpu.SemaphoreType.DMA
    vmem = pl.BlockSpec(memory_space=pltpu.VMEM)
    hbm = pl.BlockSpec(memory_space=pl.ANY)
    result = pl.pallas_call(
        functools.partial(kernel, n_lat, n_lat == 8, n_var, n_lev, n_row),
        out_shape=pltpu.VMEM((n_split, n_all, 128), F32),
        in_specs=[hbm] * 10,
        out_specs=vmem,
        scratch_shapes=[
            pltpu.VMEM(region.shape, jnp.int32),
            pltpu.VMEM(land.shape, jnp.int32),
            pltpu.VMEM(coef_table.shape[::-1], F32),
            pltpu.VMEM((1, hid), F32),
            pltpu.VMEM(b_mid.shape, F32),
            pltpu.VMEM(b_out.shape, F32),
            pltpu.VMEM(w_in.shape[::-1], BF),
            pltpu.VMEM(w_mid.shape, BF),
            pltpu.VMEM(w_out.shape, BF),
            pltpu.VMEM((hid, 2 * feat), BF),
            pltpu.VMEM((2, feat, hid), BF),
            pltpu.VMEM((n_row, feat, n_lon), BF),
            pltpu.VMEM((2, PRE, feat, n_lon), BF),
            pltpu.VMEM((PRE - 1, feat, n_lon), BF),
            pltpu.VMEM((2, 2, n_row, n_lon), jnp.int32),
            pltpu.VMEM((rows, feat, n_lon), F32),
            pltpu.VMEM((rows, feat, n_lon), F32),
            pltpu.VMEM((rows, feat, n_lon), F32),
            pltpu.VMEM((rows, feat, n_lon), F32),
            pltpu.VMEM((rows, pad_lev, n_lon), F32),
            pltpu.VMEM((rows, pad_lev, n_lon), F32),
            pltpu.VMEM((rows, pad_lev, n_lon), F32),
            pltpu.VMEM((rows, pad_lev, n_lon), F32),
            pltpu.VMEM((PRE, feat, n_lon), BF),
            pltpu.VMEM((PRE, 2 * feat, n_lon), BF),
            pltpu.VMEM((hid, n_lon), BF),
            pltpu.VMEM((hid, n_lon), BF),
            pltpu.VMEM((PRE, 2, feat, n_lon), BF),
            pltpu.VMEM((n_row + 2 * POST, feat, n_lon), BF),
            pltpu.VMEM((w_mid.shape[0] * hid + 2 * feat, 128), F32),
            dma((n_split,)),
            dma((6,)),
            dma((3,)),
            dma((2, 2)),
            dma((2, 2)),
            dma((2, PRE, 2)),
            dma((2, PRE, 2)),
            dma((PRE - 1, 2)),
            dma((PRE - 1, 2)),
            dma((PRE,)),
            dma((PRE,)),
            dma((PRE,)),
            dma((PRE,)),
            dma((POST, 2)),
            dma((2, POST)),
        ],
        compiler_params=pltpu.CompilerParams(
            collective_id=0, has_side_effects=True, vmem_limit_bytes=60 * 2**20
        ),
    )(
        region, land, coef_table.T, b_in.reshape(1, -1), b_mid, b_out,
        fields.reshape(n_all, n_lon), w_in.T, w_mid, w_out,
    )
    closure = pl.pallas_call(
        write_out,
        out_shape=jax.ShapeDtypeStruct((n_all, n_lon), F32),
        in_specs=[vmem],
        out_specs=hbm,
        scratch_shapes=[dma((n_split,))],
    )(pltpu.with_memory_space_constraint(result, pltpu.VMEM))
    return closure.reshape(fields.shape)


def solution(mesh):
    placed = (
        P(None, "lev", ("parts", "lat"), None),
        P(("parts", "lat"), None),
        P(("parts", "lat"), None),
    ) + (P(),) * 7
    return jax.shard_map(
        functools.partial(per_device, mesh.shape["lat"]),
        mesh=mesh,
        in_specs=placed,
        out_specs=P(None, "lev", ("parts", "lat"), None),
        check_vma=False,
    )
```

```python
import functools

import jax
import jax.numpy as jnp
from jax import lax
from jax.experimental import pallas as pl
from jax.experimental.pallas import tpu as pltpu
from jax.sharding import PartitionSpec as P

PRE = 4
POST = 2
MESH = pl.DeviceIdType.MESH
BF = jnp.bfloat16
F32 = jnp.float32


SCALE = 0.7978845608028654


def gelu(x):
    inner = x * (SCALE + (SCALE * 0.044715) * (x * x))
    half = 0.5 * x
    return half + half * jnp.tanh(inner)


def gelu_of_half(half):
    inner = half * (2.0 * SCALE + (8.0 * SCALE * 0.044715) * (half * half))
    return half + half * jnp.tanh(inner)


def kernel(
    n_lat, folded, n_var, n_lev, n_row,
    region_hbm, land_hbm, table_hbm, b_in_hbm, b_mid_hbm, b_out_hbm,
    fields, w_in_hbm, w_mid_hbm, w_out_hbm,
    split,
    region, land, table, b_in, b_mid, b_out, w_in, w_mid, w_out, wi, wo,
    sent, halo, passed, marks, f0, f1, f2, f3, ef, ew, nf, cf, prof, cols, h1, h2, flux_own, flux, bias,
    in_sem, small_sem, w_sem, mark_send, mark_recv, halo_send, halo_recv, passed_send, passed_recv, prof_send, prof_recv,
    flux_send, flux_recv, edge_send, edge_recv,
):
    lat = lax.axis_index("lat")
    lev = lax.axis_index("lev")
    peer = 1 - lev
    has_up = lat > 0
    has_down = lat < n_lat - 1
    odd = lat % 2
    pair = lat // 2
    n_pair = n_lat // 2
    above = pair * PRE // n_pair
    below = (n_pair - 1 - pair) * PRE // n_pair
    first_mine = PRE - jnp.where(odd == 1, below, above)
    first_passed = PRE - jnp.where(odd == 1, above, below)
    target = lat + 2 - 4 * odd
    source = lat - 2 + 4 * odd
    has_target = (target >= 0) & (target < n_lat)
    has_source = (source >= 0) & (source < n_lat)
    pad_lev = ef.shape[1]
    feat = n_var * pad_lev
    n_lon = fields.shape[1]
    hid = w_mid.shape[1]
    n_mid = w_mid.shape[0]
    half = n_row // 2
    first = PRE
    last = PRE + n_row - 1

    lanes = split.shape[2]
    n_split = split.shape[0]

    barrier = pltpu.get_barrier_semaphore()
    pl.semaphore_signal(barrier, inc=1, device_id={"lev": peer}, device_id_type=MESH)

    @pl.when(has_up)
    def _():
        for j in range(2):
            pl.semaphore_signal(
                barrier, inc=1, device_id={"lat": lat - 1, "lev": j}, device_id_type=MESH
            )

    @pl.when(has_down)
    def _():
        for j in range(2):
            pl.semaphore_signal(
                barrier, inc=1, device_id={"lat": lat + 1, "lev": j}, device_id_type=MESH
            )

    if folded:

        @pl.when(has_source)
        def _():
            pl.semaphore_signal(barrier, inc=1, device_id={"lat": source}, device_id_type=MESH)

    def columns_of(ref, c):
        return ref.at[:, c * lanes : (c + 1) * lanes]

    pieces = [
        pltpu.make_async_copy(columns_of(fields, c), split.at[c], in_sem.at[c])
        for c in range(n_split)
    ]
    for piece in pieces:
        piece.start()
    small = [
        pltpu.make_async_copy(source, target, small_sem.at[k])
        for k, (source, target) in enumerate((
            (region_hbm, region), (land_hbm, land), (table_hbm, table),
            (b_in_hbm, b_in), (b_mid_hbm, b_mid), (b_out_hbm, b_out),
        ))
    ]
    for piece in small:
        piece.start()
    loads = [
        pltpu.make_async_copy(w_in_hbm, w_in, w_sem.at[0]),
        pltpu.make_async_copy(w_out_hbm, w_out, w_sem.at[1]),
        pltpu.make_async_copy(w_mid_hbm, w_mid, w_sem.at[2]),
    ]

    def take_row(r):
        for v in range(n_var):
            base = v * n_lev * n_row
            values = jnp.concatenate(
                [split[c, pl.ds(base + r, n_lev, stride=n_row), :] for c in range(n_split)],
                axis=1,
            )
            values = jnp.concatenate(
                [values, jnp.ones((pad_lev - n_lev, n_lon), F32)], axis=0
            )
            f0[PRE + r, v * pad_lev : (v + 1) * pad_lev, :] = values
            sent[r, v * pad_lev : (v + 1) * pad_lev, :] = values.astype(BF)

    cut = feat // 2

    def row_up(k, h):
        part = pl.ds(h * cut, cut)
        return pltpu.make_async_remote_copy(
            src_ref=sent.at[k, part], dst_ref=halo.at[1, k, part],
            send_sem=halo_send.at[1, k, h], recv_sem=halo_recv.at[1, k, h],
            device_id={"lat": lat - 1}, device_id_type=MESH,
        )

    def row_down(k, h):
        part = pl.ds(h * cut, cut)
        return pltpu.make_async_remote_copy(
            src_ref=sent.at[n_row - 1 - k, part], dst_ref=halo.at[0, k, part],
            send_sem=halo_send.at[0, k, h], recv_sem=halo_recv.at[0, k, h],
            device_id={"lat": lat + 1}, device_id_type=MESH,
        )

    def by_pair(side, k):
        return (odd == 1 - side) & (k >= first_mine) if folded else lat < 0

    def to_pair(side, k, h):
        part = pl.ds(h * cut, cut)
        row = n_row - 1 - k if side == 0 else k
        return pltpu.make_async_remote_copy(
            src_ref=sent.at[row, part], dst_ref=passed.at[k - 1, part],
            send_sem=halo_send.at[side, k, h], recv_sem=passed_recv.at[k - 1, h],
            device_id={"lat": lat + 1 - 2 * odd}, device_id_type=MESH,
        )

    def pass_on(k, h):
        part = pl.ds(h * cut, cut)
        return pltpu.make_async_remote_copy(
            src_ref=passed.at[k - 1, part], dst_ref=halo.at[odd, k, part],
            send_sem=passed_send.at[k - 1, h], recv_sem=halo_recv.at[odd, k, h],
            device_id={"lat": target}, device_id_type=MESH,
        )

    def send_row(side, k, h):
        exists, row = ((has_down, row_down), (has_up, row_up))[side]

        @pl.when(exists & jnp.logical_not(by_pair(side, k)))
        def _():
            row(k, h).start()

    def send_pair(side, k):
        if folded:
            exists = (has_down, has_up)[side]

            @pl.when(exists & by_pair(side, k))
            def _():
                to_pair(side, k, 0).start()
                to_pair(side, k, 1).start()

    def marks_to(side, which, source, target):
        return pltpu.make_async_remote_copy(
            src_ref=source, dst_ref=marks.at[side, which],
            send_sem=mark_send.at[side, which], recv_sem=mark_recv.at[side, which],
            device_id={"lat": target}, device_id_type=MESH,
        )

    for piece in pieces + small:
        piece.wait()
    take_row(0)
    take_row(n_row - 1)
    for load in loads:
        load.start()

    greeted = 1 + 2 * has_up.astype(jnp.int32) + 2 * has_down.astype(jnp.int32)
    if folded:
        greeted = greeted + has_target.astype(jnp.int32)
    pl.semaphore_wait(barrier, greeted)

    @pl.when(has_up)
    def _():
        marks_to(1, 0, region, lat - 1).start()
        marks_to(1, 1, land, lat - 1).start()
        row_up(0, 0).start()
        row_up(0, 1).start()

    @pl.when(has_down)
    def _():
        marks_to(0, 0, region, lat + 1).start()
        marks_to(0, 1, land, lat + 1).start()
        row_down(0, 0).start()
        row_down(0, 1).start()

    for k in range(1, PRE):
        take_row(k)
        take_row(n_row - 1 - k)
        if k == 1:
            send_pair(1, 1)
            send_pair(0, 1)

    n_region, all_lev = table.shape
    wide = jnp.concatenate([table[...], jnp.zeros((n_region, 128 - all_lev), F32)], axis=1)
    wide = pltpu.roll(wide, (128 - lev * n_lev) % 128, 1)
    wide = jnp.concatenate([wide] * (128 // n_region), axis=0).T[:pad_lev]
    level_id = lax.broadcasted_iota(jnp.int32, (pad_lev, 128), 0)
    wide = jnp.where(level_id < n_lev, wide, 0.0)
    columns = [
        jnp.broadcast_to(wide[:, k : k + 1], (pad_lev, n_lon)) for k in range(n_region)
    ]

    def coefficient(region_row, land_row):
        region_row = jnp.broadcast_to(region_row, (pad_lev, n_lon))
        total = columns[0]
        for k in range(1, len(columns)):
            total = jnp.where(region_row == k, columns[k], total)
        return total * (1.0 - 0.6 * land_row.astype(F32))

    for r in range(n_row):
        ef[first + r] = coefficient(region[r : r + 1, :], land[r : r + 1, :])

    def faces_north(i):
        nf[i] = jnp.sqrt(ef[i] * ef[i + 1])

    def faces_east(i):
        c = ef[i]
        east = jnp.sqrt(c * pltpu.roll(c, n_lon - 1, 1))
        ef[i] = east
        ew[i] = pltpu.roll(east, 1, 1)

    for i in range(first, last):
        faces_north(i)

    def centre(i):
        cf[i] = 1.0 - ((ef[i] + ew[i]) + (nf[i] + nf[i - 1]))

    def step_rows(src, dst, i, store=None):
        size = 16
        for s in range(0, pad_lev, size):
            own = cf[i, s : s + size, :]
            east = ef[i, s : s + size, :]
            west = ew[i, s : s + size, :]
            north = nf[i, s : s + size, :]
            south = nf[i - 1, s : s + size, :]
            for v in range(n_var):
                rows = slice(v * pad_lev + s, v * pad_lev + s + size)
                f = src[i, rows, :]
                near = f.astype(BF)
                zonal = east * pltpu.roll(near, n_lon - 1, 1).astype(F32)
                zonal = zonal + west * pltpu.roll(near, 1, 1).astype(F32)
                meridional = north * src[i + 1, rows, :] + south * src[i - 1, rows, :]
                value = (own * f + zonal) + meridional
                if store is None:
                    dst[i, rows, :] = value
                else:
                    store(v, s, rows, value)

    def loop_rows(low, high, fn):
        def body(i, carry):
            fn(i)
            return carry

        lax.fori_loop(low, high, body, 0)

    for side in range(2):
        exists = has_up if side == 0 else has_down

        @pl.when(exists)
        def _():
            for which in range(2):
                marks_to(side, which, region, lat).wait_recv()
            for k in range(PRE):
                r = n_row - 1 - k if side == 0 else k
                i = first - 1 - k if side == 0 else last + 1 + k
                ef[i] = coefficient(
                    marks[side, 0, r : r + 1, :], marks[side, 1, r : r + 1, :]
                )

        @pl.when(jnp.logical_not(exists))
        def _():
            for k in range(PRE):
                i = first - 1 - k if side == 0 else last + 1 + k
                ef[i] = jnp.zeros((pad_lev, n_lon), F32)
                f0[i] = jnp.zeros((feat, n_lon), F32)

    for i in list(range(0, first)) + list(range(last, last + PRE)):
        faces_north(i)
    for i in range(0, last + PRE + 1):
        faces_east(i)
    for i in range(1, last + PRE):
        centre(i)

    send_row(1, 1, 0)
    send_row(0, 1, 0)

    loop_rows(first + 1, last, lambda i: step_rows(f0, f1, i))
    loop_rows(first + 2, last - 1, lambda i: step_rows(f1, f2, i))
    loop_rows(first + 3, last - 2, lambda i: step_rows(f2, f3, i))

    loads[0].wait()
    loads[1].wait()
    n_feat = w_out.shape[0]
    f_id = lax.broadcasted_iota(jnp.int32, (feat, n_feat), 1)
    c_id = lax.broadcasted_iota(jnp.int32, (feat, n_feat), 0)
    l_id = c_id % pad_lev
    half_b = 0.5 * b_in[...]
    b_parts = []
    for _ in range(3):
        b_parts.append(half_b.astype(BF))
        half_b = half_b - b_parts[-1].astype(F32)
    place_id = lax.broadcasted_iota(jnp.int32, (feat, hid), 0)
    for j in range(2):
        want = (c_id // pad_lev) * (2 * n_lev) + j * n_lev + l_id
        found = (f_id == want) & (l_id < n_lev)
        halves = jnp.where(found, 0.5, 0.0).astype(BF)
        weight = jnp.dot(halves, w_in[...], preferred_element_type=F32)
        if j == 0:
            for place, part in zip((n_lev, n_lev + 1, pad_lev + n_lev), b_parts):
                weight = jnp.where(place_id == place, part.astype(F32), weight)
        wi[:, j * feat : (j + 1) * feat] = weight.T.astype(BF)
        pick = jnp.where(found, 1.0, 0.0).astype(BF)
        wo[j] = jnp.dot(pick, w_out[...], preferred_element_type=F32).astype(BF)

    def tall(row):
        return jnp.broadcast_to(row, (128, 128)).T

    start = n_mid * hid
    for m in range(0, n_feat, 128):
        count = min(128, n_feat - m)
        row = b_out[m : m + count].reshape(1, count)
        if count < 128:
            row = jnp.concatenate([row, jnp.zeros((1, 128 - count), F32)], axis=1)
        bias[m : m + 128, :] = tall(row)
    bias[start : start + 2 * feat, :] = jnp.zeros((2 * feat, 128), F32)
    for v in range(n_var):
        for j in range(2):
            place = start + j * feat + v * pad_lev
            origin = v * 2 * n_lev + j * n_lev
            bias[place : place + n_lev, :] = bias[origin : origin + n_lev, :]
    for m in range(0, hid, 128):
        for layer in range(n_mid):
            start = layer * hid + m
            bias[start : start + 128, :] = tall(b_mid[layer : layer + 1, m : m + 128])
    loads[2].wait()

    tile = 256

    def with_bias(x, start, size):
        b = bias[start : start + size, :]
        return x + jnp.concatenate([b] * (n_lon // b.shape[1]), axis=1)

    def profile_copy(p):
        return pltpu.make_async_remote_copy(
            src_ref=prof.at[p], dst_ref=cols.at[p, pl.ds(lev * feat, feat)],
            send_sem=prof_send.at[p], recv_sem=prof_recv.at[p],
            device_id={"lev": peer}, device_id_type=MESH,
        )

    def flux_row(owner, p):
        return half - 1 - p + owner * (1 + 2 * p)

    def flux_copy(p):
        return pltpu.make_async_remote_copy(
            src_ref=flux_own.at[p, peer], dst_ref=flux.at[flux_row(lev, p) + POST],
            send_sem=flux_send.at[p], recv_sem=flux_recv.at[p],
            device_id={"lev": peer}, device_id_type=MESH,
        )

    def edge_copy(p, j):
        q = p - (half - POST)
        place = flux_row(lev, p) + POST + (1 - 2 * lev) * n_row
        return pltpu.make_async_remote_copy(
            src_ref=flux_own.at[p, j], dst_ref=flux.at[place],
            send_sem=edge_send.at[q, j], recv_sem=edge_recv.at[peer, q],
            device_id={"lat": lat - 1 + 2 * lev, "lev": j}, device_id_type=MESH,
        )

    has_edge = jnp.where(lev == 0, has_up, has_down)

    def smooth(p, side, store):
        @pl.when(jnp.where(side == 0, has_up, has_down))
        def _():
            for h in range(2):
                part = pl.ds(h * cut, cut)
                pltpu.make_async_remote_copy(
                    src_ref=sent.at[0, part], dst_ref=halo.at[side, p, part],
                    send_sem=halo_send.at[side, p, h], recv_sem=halo_recv.at[side, p, h],
                    device_id={"lev": peer}, device_id_type=MESH,
                ).wait_recv()
            f0[jnp.where(side == 0, first - 1 - p, last + 1 + p)] = halo[side, p].astype(F32)

        for k, (src, dst) in enumerate(((f0, f1), (f1, f2), (f2, f3), (f3, None))):
            at = jnp.where(side == 0, first - p + k, last + p - k)
            step_rows(src, dst, at, store if dst is None else None)

    def phase(p, carry):
        def save_peer(v, s, rows, value):
            prof[p, rows, :] = value.astype(BF)

        def save_own(v, s, rows, value):
            place = pl.multiple_of(lev * feat + rows.start, 16)
            cols[p, pl.ds(place, rows.stop - rows.start), :] = value.astype(BF)

        smooth(p, peer, save_peer)
        exchange = profile_copy(p)
        exchange.start()
        smooth(p, lev, save_own)

        @pl.when(p < PRE - 1)
        def _():
            for side in (1, 0):
                send_row(side, p + 1, 1)

        @pl.when(p < PRE - 2)
        def _():
            for side in (1, 0):
                send_pair(side, p + 2)

        @pl.when(has_edge & (p > half - POST))
        def _():
            edge_copy(p - 1, 1).start()

        if folded:

            @pl.when(has_target & (p < PRE - 1) & (p + 1 >= first_passed))
            def _():
                for h in range(2):
                    to_pair(0, p + 1, h).wait_recv()
                    pass_on(p + 1, h).start()

        pltpu.make_async_remote_copy(
            src_ref=prof.at[p], dst_ref=cols.at[p, pl.ds(peer * feat, feat)],
            send_sem=prof_send.at[p], recv_sem=prof_recv.at[p],
            device_id={"lev": peer}, device_id_type=MESH,
        ).wait_recv()

        for m in range(0, hid, tile):
            x = jnp.dot(wi[m : m + tile, :], cols[p], preferred_element_type=F32)
            h1[m : m + tile, :] = gelu_of_half(x).astype(BF)
        now, then = h1, h2
        for layer in range(n_mid):
            for m in range(0, hid, tile):
                x = jnp.dot(w_mid[layer, m : m + tile, :], now[...], preferred_element_type=F32)
                x = with_bias(x, layer * hid + m, tile)
                then[m : m + tile, :] = gelu(x).astype(BF)
            now, then = then, now
        for j in range(2):
            x = jnp.dot(wo[j], now[...], preferred_element_type=F32)
            flux_own[p, j] = with_bias(x, n_mid * hid + j * feat, feat).astype(BF)
        @pl.when(p < PRE - 2)
        def _():
            for side in (1, 0):
                send_row(side, p + 2, 0)

        flux[flux_row(lev, p) + POST] = flux_own[p, lev]
        flux_copy(p).start()

        @pl.when(has_edge & (p >= half - POST))
        def _():
            edge_copy(p, 0).start()

        return carry

    lax.fori_loop(0, PRE, phase, 0)

    @pl.when(has_edge)
    def _():
        edge_copy(half - 1, 1).start()

    for p in range(half):
        flux_copy(p).wait_recv()

    def widen(i):
        f0[i] = flux[i - PRE + POST].astype(F32)

    loop_rows(first, last + 1, widen)

    def finish(i):
        def store(v, s, rows, value):
            count = min(16, n_lev - s)
            base = v * (n_lev * n_row) + s * n_row + (i - first)
            for c in range(n_split):
                split[c, pl.ds(base, count, stride=n_row), :] = value[
                    :count, c * lanes : (c + 1) * lanes
                ]

        step_rows(f1, None, i, store)

    loop_rows(first + 1, last, lambda i: step_rows(f0, f1, i))
    loop_rows(first + 2, last - 1, finish)

    for side in range(2):
        exists = has_up if side == 0 else has_down

        @pl.when(exists)
        def _():
            for q in range(POST):
                pltpu.make_async_remote_copy(
                    src_ref=flux_own.at[0, 0], dst_ref=flux.at[0],
                    send_sem=edge_send.at[0, 0], recv_sem=edge_recv.at[side, q],
                    device_id={"lev": peer}, device_id_type=MESH,
                ).wait_recv()
            for q in range(POST):
                widen(first - 1 - q if side == 0 else last + 1 + q)

    for i in (first - 1, first, last, last + 1):
        step_rows(f0, f1, i)
    for i in (first, first + 1, last - 1, last):
        finish(i)
    for k in range(PRE):
        profile_copy(k).wait_send()
        flux_copy(k).wait_send()

    @pl.when(has_up)
    def _():
        for which in range(2):
            marks_to(1, which, region, lat).wait_send()
        for k in range(PRE):
            row_up(k, 0).wait_send()
            row_up(k, 1).wait_send()

    @pl.when(has_down)
    def _():
        for which in range(2):
            marks_to(0, which, region, lat).wait_send()
        for k in range(PRE):
            row_down(k, 0).wait_send()
            row_down(k, 1).wait_send()

    if folded:
        for k in range(1, PRE):

            @pl.when(has_target & (k >= first_passed))
            def _():
                for h in range(2):
                    pass_on(k, h).wait_send()

    @pl.when(has_edge)
    def _():
        for p in range(half - POST, half):
            for j in range(2):
                edge_copy(p, j).wait_send()


def write_out(split, out, sem):
    lanes = split.shape[2]
    pieces = [
        pltpu.make_async_copy(split.at[c], out.at[:, c * lanes : (c + 1) * lanes], sem.at[c])
        for c in range(split.shape[0])
    ]
    for piece in pieces:
        piece.start()
    for piece in pieces:
        piece.wait()


def per_device(n_lat, fields, region, land, coef_table, w_in, b_in, w_mid, b_mid, w_out, b_out):
    n_var, n_lev, n_row, n_lon = fields.shape
    hid = w_in.shape[0]
    pad_lev = -(-n_lev // 16) * 16
    feat = n_var * pad_lev
    rows = n_row + 2 * PRE
    n_split = n_lon // 128
    n_all = n_var * n_lev * n_row
    dma = pltpu.SemaphoreType.DMA
    vmem = pl.BlockSpec(memory_space=pltpu.VMEM)
    hbm = pl.BlockSpec(memory_space=pl.ANY)
    result = pl.pallas_call(
        functools.partial(kernel, n_lat, n_lat == 8, n_var, n_lev, n_row),
        out_shape=pltpu.VMEM((n_split, n_all, 128), F32),
        in_specs=[hbm] * 10,
        out_specs=vmem,
        scratch_shapes=[
            pltpu.VMEM(region.shape, jnp.int32),
            pltpu.VMEM(land.shape, jnp.int32),
            pltpu.VMEM(coef_table.shape[::-1], F32),
            pltpu.VMEM((1, hid), F32),
            pltpu.VMEM(b_mid.shape, F32),
            pltpu.VMEM(b_out.shape, F32),
            pltpu.VMEM(w_in.shape[::-1], BF),
            pltpu.VMEM(w_mid.shape, BF),
            pltpu.VMEM(w_out.shape, BF),
            pltpu.VMEM((hid, 2 * feat), BF),
            pltpu.VMEM((2, feat, hid), BF),
            pltpu.VMEM((n_row, feat, n_lon), BF),
            pltpu.VMEM((2, PRE, feat, n_lon), BF),
            pltpu.VMEM((PRE - 1, feat, n_lon), BF),
            pltpu.VMEM((2, 2, n_row, n_lon), jnp.int32),
            pltpu.VMEM((rows, feat, n_lon), F32),
            pltpu.VMEM((rows, feat, n_lon), F32),
            pltpu.VMEM((rows, feat, n_lon), F32),
            pltpu.VMEM((rows, feat, n_lon), F32),
            pltpu.VMEM((rows, pad_lev, n_lon), F32),
            pltpu.VMEM((rows, pad_lev, n_lon), F32),
            pltpu.VMEM((rows, pad_lev, n_lon), F32),
            pltpu.VMEM((rows, pad_lev, n_lon), F32),
            pltpu.VMEM((PRE, feat, n_lon), BF),
            pltpu.VMEM((PRE, 2 * feat, n_lon), BF),
            pltpu.VMEM((hid, n_lon), BF),
            pltpu.VMEM((hid, n_lon), BF),
            pltpu.VMEM((PRE, 2, feat, n_lon), BF),
            pltpu.VMEM((n_row + 2 * POST, feat, n_lon), BF),
            pltpu.VMEM((w_mid.shape[0] * hid + 2 * feat, 128), F32),
            dma((n_split,)),
            dma((6,)),
            dma((3,)),
            dma((2, 2)),
            dma((2, 2)),
            dma((2, PRE, 2)),
            dma((2, PRE, 2)),
            dma((PRE - 1, 2)),
            dma((PRE - 1, 2)),
            dma((PRE,)),
            dma((PRE,)),
            dma((PRE,)),
            dma((PRE,)),
            dma((POST, 2)),
            dma((2, POST)),
        ],
        compiler_params=pltpu.CompilerParams(
            collective_id=0, has_side_effects=True, vmem_limit_bytes=60 * 2**20
        ),
    )(
        region, land, coef_table.T, b_in.reshape(1, -1), b_mid, b_out,
        fields.reshape(n_all, n_lon), w_in.T, w_mid, w_out,
    )
    closure = pl.pallas_call(
        write_out,
        out_shape=jax.ShapeDtypeStruct((n_all, n_lon), F32),
        in_specs=[vmem],
        out_specs=hbm,
        scratch_shapes=[dma((n_split,))],
    )(pltpu.with_memory_space_constraint(result, pltpu.VMEM))
    return closure.reshape(fields.shape)


def solution(mesh):
    placed = (
        P(None, "lev", ("parts", "lat"), None),
        P(("parts", "lat"), None),
        P(("parts", "lat"), None),
    ) + (P(),) * 7
    return jax.shard_map(
        functools.partial(per_device, mesh.shape["lat"]),
        mesh=mesh,
        in_specs=placed,
        out_specs=P(None, "lev", ("parts", "lat"), None),
        check_vma=False,
    )
```

```python
import functools

import jax
import jax.numpy as jnp
from jax import lax
from jax.experimental import pallas as pl
from jax.experimental.pallas import tpu as pltpu
from jax.sharding import PartitionSpec as P

PRE = 4
POST = 2
MESH = pl.DeviceIdType.MESH
BF = jnp.bfloat16
F32 = jnp.float32


SCALE = 0.7978845608028654


def gelu(x):
    inner = x * (SCALE + (SCALE * 0.044715) * (x * x))
    half = 0.5 * x
    return half + half * jnp.tanh(inner)


def gelu_of_half(half):
    inner = half * (2.0 * SCALE + (8.0 * SCALE * 0.044715) * (half * half))
    return half + half * jnp.tanh(inner)


def kernel(
    n_lat, folded, n_var, n_lev, n_row,
    region_hbm, land_hbm, table_hbm, b_in_hbm, b_mid_hbm, b_out_hbm,
    fields, w_in_hbm, w_mid_hbm, w_out_hbm,
    split,
    region, land, table, b_in, b_mid, b_out, w_in, w_mid, w_out, wi, wo,
    sent, halo, passed, code, marks, f0, f1, f2, f3, ef, ew, nf, cf, prof, cols, h1, h2, flux_own, flux, bias,
    in_sem, small_sem, w_sem, mark_send, mark_recv, halo_send, halo_recv, passed_send, passed_recv, prof_send, prof_recv,
    flux_send, flux_recv, edge_send, edge_recv,
):
    lat = lax.axis_index("lat")
    lev = lax.axis_index("lev")
    peer = 1 - lev
    has_up = lat > 0
    has_down = lat < n_lat - 1
    odd = lat % 2
    pair = lat // 2
    n_pair = n_lat // 2
    above = pair * PRE // n_pair
    below = (n_pair - 1 - pair) * PRE // n_pair
    first_mine = PRE - jnp.where(odd == 1, below, above)
    first_passed = PRE - jnp.where(odd == 1, above, below)
    target = lat + 2 - 4 * odd
    source = lat - 2 + 4 * odd
    has_target = (target >= 0) & (target < n_lat)
    has_source = (source >= 0) & (source < n_lat)
    pad_lev = ef.shape[1]
    feat = n_var * pad_lev
    n_lon = fields.shape[1]
    hid = w_mid.shape[1]
    n_mid = w_mid.shape[0]
    n_region, all_lev = table.shape
    half = n_row // 2
    first = PRE
    last = PRE + n_row - 1

    lanes = split.shape[2]
    n_split = split.shape[0]

    barrier = pltpu.get_barrier_semaphore()
    pl.semaphore_signal(barrier, inc=1, device_id={"lev": peer}, device_id_type=MESH)

    @pl.when(has_up)
    def _():
        for j in range(2):
            pl.semaphore_signal(
                barrier, inc=1, device_id={"lat": lat - 1, "lev": j}, device_id_type=MESH
            )

    @pl.when(has_down)
    def _():
        for j in range(2):
            pl.semaphore_signal(
                barrier, inc=1, device_id={"lat": lat + 1, "lev": j}, device_id_type=MESH
            )

    if folded:

        @pl.when(has_source)
        def _():
            pl.semaphore_signal(barrier, inc=1, device_id={"lat": source}, device_id_type=MESH)

    def columns_of(ref, c):
        return ref.at[:, c * lanes : (c + 1) * lanes]

    pieces = [
        pltpu.make_async_copy(columns_of(fields, c), split.at[c], in_sem.at[c])
        for c in range(n_split)
    ]
    for piece in pieces:
        piece.start()
    small = [
        pltpu.make_async_copy(source, target, small_sem.at[k])
        for k, (source, target) in enumerate((
            (region_hbm, region), (land_hbm, land), (table_hbm, table),
            (b_in_hbm, b_in), (b_mid_hbm, b_mid), (b_out_hbm, b_out),
        ))
    ]
    for piece in small:
        piece.start()
    loads = [
        pltpu.make_async_copy(w_in_hbm, w_in, w_sem.at[0]),
        pltpu.make_async_copy(w_out_hbm, w_out, w_sem.at[1]),
        pltpu.make_async_copy(w_mid_hbm, w_mid, w_sem.at[2]),
    ]

    def take_row(r):
        for v in range(n_var):
            base = v * n_lev * n_row
            values = jnp.concatenate(
                [split[c, pl.ds(base + r, n_lev, stride=n_row), :] for c in range(n_split)],
                axis=1,
            )
            values = jnp.concatenate(
                [values, jnp.ones((pad_lev - n_lev, n_lon), F32)], axis=0
            )
            f0[PRE + r, v * pad_lev : (v + 1) * pad_lev, :] = values
            sent[r, v * pad_lev : (v + 1) * pad_lev, :] = values.astype(BF)

    cut = feat // 2

    def row_up(k, h):
        part = pl.ds(h * cut, cut)
        return pltpu.make_async_remote_copy(
            src_ref=sent.at[k, part], dst_ref=halo.at[1, k, part],
            send_sem=halo_send.at[1, k, h], recv_sem=halo_recv.at[1, k, h],
            device_id={"lat": lat - 1}, device_id_type=MESH,
        )

    def row_down(k, h):
        part = pl.ds(h * cut, cut)
        return pltpu.make_async_remote_copy(
            src_ref=sent.at[n_row - 1 - k, part], dst_ref=halo.at[0, k, part],
            send_sem=halo_send.at[0, k, h], recv_sem=halo_recv.at[0, k, h],
            device_id={"lat": lat + 1}, device_id_type=MESH,
        )

    def by_pair(side, k):
        return (odd == 1 - side) & (k >= first_mine) if folded else lat < 0

    def to_pair(side, k, h):
        part = pl.ds(h * cut, cut)
        row = n_row - 1 - k if side == 0 else k
        return pltpu.make_async_remote_copy(
            src_ref=sent.at[row, part], dst_ref=passed.at[k - 1, part],
            send_sem=halo_send.at[side, k, h], recv_sem=passed_recv.at[k - 1, h],
            device_id={"lat": lat + 1 - 2 * odd}, device_id_type=MESH,
        )

    def pass_on(k, h):
        part = pl.ds(h * cut, cut)
        return pltpu.make_async_remote_copy(
            src_ref=passed.at[k - 1, part], dst_ref=halo.at[odd, k, part],
            send_sem=passed_send.at[k - 1, h], recv_sem=halo_recv.at[odd, k, h],
            device_id={"lat": target}, device_id_type=MESH,
        )

    def send_row(side, k, h):
        exists, row = ((has_down, row_down), (has_up, row_up))[side]

        @pl.when(exists & jnp.logical_not(by_pair(side, k)))
        def _():
            row(k, h).start()

    def send_pair(side, k):
        if folded:
            exists = (has_down, has_up)[side]

            @pl.when(exists & by_pair(side, k))
            def _():
                to_pair(side, k, 0).start()
                to_pair(side, k, 1).start()

    def marks_to(side, target):
        part = pl.ds(0, PRE) if side == 1 else pl.ds(n_row - PRE, PRE)
        return pltpu.make_async_remote_copy(
            src_ref=code.at[part], dst_ref=marks.at[side, part],
            send_sem=mark_send.at[side], recv_sem=mark_recv.at[side],
            device_id={"lat": target}, device_id_type=MESH,
        )

    for piece in pieces + small:
        piece.wait()
    code[...] = region[...] + n_region * land[...]
    take_row(0)
    take_row(n_row - 1)
    for load in loads:
        load.start()

    greeted = 1 + 2 * has_up.astype(jnp.int32) + 2 * has_down.astype(jnp.int32)
    if folded:
        greeted = greeted + has_target.astype(jnp.int32)
    pl.semaphore_wait(barrier, greeted)

    @pl.when(has_up)
    def _():
        marks_to(1, lat - 1).start()
        row_up(0, 0).start()
        row_up(0, 1).start()

    @pl.when(has_down)
    def _():
        marks_to(0, lat + 1).start()
        row_down(0, 0).start()
        row_down(0, 1).start()

    for k in range(1, PRE):
        take_row(k)
        take_row(n_row - 1 - k)
        if k == 1:
            send_pair(1, 1)
            send_pair(0, 1)

    wide = jnp.concatenate([table[...], jnp.zeros((n_region, 128 - all_lev), F32)], axis=1)
    wide = pltpu.roll(wide, (128 - lev * n_lev) % 128, 1)
    wide = jnp.concatenate([wide] * (128 // n_region), axis=0).T[:pad_lev]
    level_id = lax.broadcasted_iota(jnp.int32, (pad_lev, 128), 0)
    wide = jnp.where(level_id < n_lev, wide, 0.0)
    columns = [
        jnp.broadcast_to(wide[:, k : k + 1], (pad_lev, n_lon)) for k in range(n_region)
    ]

    def coefficient(region_row, land_row):
        region_row = jnp.broadcast_to(region_row, (pad_lev, n_lon))
        total = columns[0]
        for k in range(1, len(columns)):
            total = jnp.where(region_row == k, columns[k], total)
        return total * (1.0 - 0.6 * land_row.astype(F32))

    for r in range(n_row):
        ef[first + r] = coefficient(region[r : r + 1, :], land[r : r + 1, :])

    def faces_north(i):
        nf[i] = jnp.sqrt(ef[i] * ef[i + 1])

    def faces_east(i):
        c = ef[i]
        east = jnp.sqrt(c * pltpu.roll(c, n_lon - 1, 1))
        ef[i] = east
        ew[i] = pltpu.roll(east, 1, 1)

    for i in range(first, last):
        faces_north(i)

    def centre(i):
        cf[i] = 1.0 - ((ef[i] + ew[i]) + (nf[i] + nf[i - 1]))

    def step_rows(src, dst, i, store=None):
        size = 16
        for s in range(0, pad_lev, size):
            own = cf[i, s : s + size, :]
            east = ef[i, s : s + size, :]
            west = ew[i, s : s + size, :]
            north = nf[i, s : s + size, :]
            south = nf[i - 1, s : s + size, :]
            for v in range(n_var):
                rows = slice(v * pad_lev + s, v * pad_lev + s + size)
                f = src[i, rows, :]
                near = f.astype(BF)
                zonal = east * pltpu.roll(near, n_lon - 1, 1).astype(F32)
                zonal = zonal + west * pltpu.roll(near, 1, 1).astype(F32)
                meridional = north * src[i + 1, rows, :] + south * src[i - 1, rows, :]
                value = (own * f + zonal) + meridional
                if store is None:
                    dst[i, rows, :] = value
                else:
                    store(v, s, rows, value)

    def loop_rows(low, high, fn):
        def body(i, carry):
            fn(i)
            return carry

        lax.fori_loop(low, high, body, 0)

    for side in range(2):
        exists = has_up if side == 0 else has_down

        @pl.when(exists)
        def _():
            marks_to(side, lat - 1 + 2 * side).wait_recv()
            for k in range(PRE):
                r = n_row - 1 - k if side == 0 else k
                i = first - 1 - k if side == 0 else last + 1 + k
                mark = marks[side, r : r + 1, :]
                is_land = jnp.where(mark >= n_region, 1, 0)
                ef[i] = coefficient(mark - n_region * is_land, is_land)

        @pl.when(jnp.logical_not(exists))
        def _():
            for k in range(PRE):
                i = first - 1 - k if side == 0 else last + 1 + k
                ef[i] = jnp.zeros((pad_lev, n_lon), F32)
                f0[i] = jnp.zeros((feat, n_lon), F32)

    for i in list(range(0, first)) + list(range(last, last + PRE)):
        faces_north(i)
    for i in range(0, last + PRE + 1):
        faces_east(i)
    for i in range(1, last + PRE):
        centre(i)

    send_row(1, 1, 0)
    send_row(0, 1, 0)

    loop_rows(first + 1, last, lambda i: step_rows(f0, f1, i))
    loop_rows(first + 2, last - 1, lambda i: step_rows(f1, f2, i))
    loop_rows(first + 3, last - 2, lambda i: step_rows(f2, f3, i))

    loads[0].wait()
    loads[1].wait()
    n_feat = w_out.shape[0]
    f_id = lax.broadcasted_iota(jnp.int32, (feat, n_feat), 1)
    c_id = lax.broadcasted_iota(jnp.int32, (feat, n_feat), 0)
    l_id = c_id % pad_lev
    half_b = 0.5 * b_in[...]
    b_parts = []
    for _ in range(3):
        b_parts.append(half_b.astype(BF))
        half_b = half_b - b_parts[-1].astype(F32)
    place_id = lax.broadcasted_iota(jnp.int32, (feat, hid), 0)
    for j in range(2):
        want = (c_id // pad_lev) * (2 * n_lev) + j * n_lev + l_id
        found = (f_id == want) & (l_id < n_lev)
        halves = jnp.where(found, 0.5, 0.0).astype(BF)
        weight = jnp.dot(halves, w_in[...], preferred_element_type=F32)
        if j == 0:
            for place, part in zip((n_lev, n_lev + 1, pad_lev + n_lev), b_parts):
                weight = jnp.where(place_id == place, part.astype(F32), weight)
        wi[:, j * feat : (j + 1) * feat] = weight.T.astype(BF)
        pick = jnp.where(found, 1.0, 0.0).astype(BF)
        wo[j] = jnp.dot(pick, w_out[...], preferred_element_type=F32).astype(BF)

    def tall(row):
        return jnp.broadcast_to(row, (128, 128)).T

    start = n_mid * hid
    for m in range(0, n_feat, 128):
        count = min(128, n_feat - m)
        row = b_out[m : m + count].reshape(1, count)
        if count < 128:
            row = jnp.concatenate([row, jnp.zeros((1, 128 - count), F32)], axis=1)
        bias[m : m + 128, :] = tall(row)
    bias[start : start + 2 * feat, :] = jnp.zeros((2 * feat, 128), F32)
    for v in range(n_var):
        for j in range(2):
            place = start + j * feat + v * pad_lev
            origin = v * 2 * n_lev + j * n_lev
            bias[place : place + n_lev, :] = bias[origin : origin + n_lev, :]
    for m in range(0, hid, 128):
        for layer in range(n_mid):
            start = layer * hid + m
            bias[start : start + 128, :] = tall(b_mid[layer : layer + 1, m : m + 128])
    loads[2].wait()

    tile = 256

    def with_bias(x, start, size):
        b = bias[start : start + size, :]
        return x + jnp.concatenate([b] * (n_lon // b.shape[1]), axis=1)

    def profile_copy(p):
        return pltpu.make_async_remote_copy(
            src_ref=prof.at[p], dst_ref=cols.at[p, pl.ds(lev * feat, feat)],
            send_sem=prof_send.at[p], recv_sem=prof_recv.at[p],
            device_id={"lev": peer}, device_id_type=MESH,
        )

    def flux_row(owner, p):
        return half - 1 - p + owner * (1 + 2 * p)

    def flux_copy(p):
        return pltpu.make_async_remote_copy(
            src_ref=flux_own.at[p, peer], dst_ref=flux.at[flux_row(lev, p) + POST],
            send_sem=flux_send.at[p], recv_sem=flux_recv.at[p],
            device_id={"lev": peer}, device_id_type=MESH,
        )

    def edge_copy(p, j):
        q = p - (half - POST)
        place = flux_row(lev, p) + POST + (1 - 2 * lev) * n_row
        return pltpu.make_async_remote_copy(
            src_ref=flux_own.at[p, j], dst_ref=flux.at[place],
            send_sem=edge_send.at[q, j], recv_sem=edge_recv.at[peer, q],
            device_id={"lat": lat - 1 + 2 * lev, "lev": j}, device_id_type=MESH,
        )

    has_edge = jnp.where(lev == 0, has_up, has_down)

    def smooth(p, side, store):
        @pl.when(jnp.where(side == 0, has_up, has_down))
        def _():
            for h in range(2):
                part = pl.ds(h * cut, cut)
                pltpu.make_async_remote_copy(
                    src_ref=sent.at[0, part], dst_ref=halo.at[side, p, part],
                    send_sem=halo_send.at[side, p, h], recv_sem=halo_recv.at[side, p, h],
                    device_id={"lev": peer}, device_id_type=MESH,
                ).wait_recv()
            f0[jnp.where(side == 0, first - 1 - p, last + 1 + p)] = halo[side, p].astype(F32)

        for k, (src, dst) in enumerate(((f0, f1), (f1, f2), (f2, f3), (f3, None))):
            at = jnp.where(side == 0, first - p + k, last + p - k)
            step_rows(src, dst, at, store if dst is None else None)

    def phase(p, carry):
        def save_peer(v, s, rows, value):
            prof[p, rows, :] = value.astype(BF)

        def save_own(v, s, rows, value):
            place = pl.multiple_of(lev * feat + rows.start, 16)
            cols[p, pl.ds(place, rows.stop - rows.start), :] = value.astype(BF)

        smooth(p, peer, save_peer)
        exchange = profile_copy(p)
        exchange.start()
        smooth(p, lev, save_own)

        @pl.when(p < PRE - 1)
        def _():
            for side in (1, 0):
                send_row(side, p + 1, 1)

        @pl.when(p < PRE - 2)
        def _():
            for side in (1, 0):
                send_pair(side, p + 2)

        @pl.when(has_edge & (p > half - POST))
        def _():
            edge_copy(p - 1, 1).start()

        if folded:

            @pl.when(has_target & (p < PRE - 1) & (p + 1 >= first_passed))
            def _():
                for h in range(2):
                    to_pair(0, p + 1, h).wait_recv()
                    pass_on(p + 1, h).start()

        pltpu.make_async_remote_copy(
            src_ref=prof.at[p], dst_ref=cols.at[p, pl.ds(peer * feat, feat)],
            send_sem=prof_send.at[p], recv_sem=prof_recv.at[p],
            device_id={"lev": peer}, device_id_type=MESH,
        ).wait_recv()

        for m in range(0, hid, tile):
            x = jnp.dot(wi[m : m + tile, :], cols[p], preferred_element_type=F32)
            h1[m : m + tile, :] = gelu_of_half(x).astype(BF)
        now, then = h1, h2
        for layer in range(n_mid):
            for m in range(0, hid, tile):
                x = jnp.dot(w_mid[layer, m : m + tile, :], now[...], preferred_element_type=F32)
                x = with_bias(x, layer * hid + m, tile)
                then[m : m + tile, :] = gelu(x).astype(BF)
            now, then = then, now
        for j in range(2):
            x = jnp.dot(wo[j], now[...], preferred_element_type=F32)
            flux_own[p, j] = with_bias(x, n_mid * hid + j * feat, feat).astype(BF)
        @pl.when(p < PRE - 2)
        def _():
            for side in (1, 0):
                send_row(side, p + 2, 0)

        flux[flux_row(lev, p) + POST] = flux_own[p, lev]
        flux_copy(p).start()

        @pl.when(has_edge & (p >= half - POST))
        def _():
            edge_copy(p, 0).start()

        return carry

    lax.fori_loop(0, PRE, phase, 0)

    @pl.when(has_edge)
    def _():
        edge_copy(half - 1, 1).start()

    for p in range(half):
        flux_copy(p).wait_recv()

    def widen(i):
        f0[i] = flux[i - PRE + POST].astype(F32)

    loop_rows(first, last + 1, widen)

    def finish(i):
        def store(v, s, rows, value):
            count = min(16, n_lev - s)
            base = v * (n_lev * n_row) + s * n_row + (i - first)
            for c in range(n_split):
                split[c, pl.ds(base, count, stride=n_row), :] = value[
                    :count, c * lanes : (c + 1) * lanes
                ]

        step_rows(f1, None, i, store)

    loop_rows(first + 1, last, lambda i: step_rows(f0, f1, i))
    loop_rows(first + 2, last - 1, finish)

    for side in range(2):
        exists = has_up if side == 0 else has_down

        @pl.when(exists)
        def _():
            for q in range(POST):
                pltpu.make_async_remote_copy(
                    src_ref=flux_own.at[0, 0], dst_ref=flux.at[0],
                    send_sem=edge_send.at[0, 0], recv_sem=edge_recv.at[side, q],
                    device_id={"lev": peer}, device_id_type=MESH,
                ).wait_recv()
            for q in range(POST):
                widen(first - 1 - q if side == 0 else last + 1 + q)

    for i in (first - 1, first, last, last + 1):
        step_rows(f0, f1, i)
    for i in (first, first + 1, last - 1, last):
        finish(i)
    for k in range(PRE):
        profile_copy(k).wait_send()
        flux_copy(k).wait_send()

    @pl.when(has_up)
    def _():
        marks_to(1, lat - 1).wait_send()
        for k in range(PRE):
            row_up(k, 0).wait_send()
            row_up(k, 1).wait_send()

    @pl.when(has_down)
    def _():
        marks_to(0, lat + 1).wait_send()
        for k in range(PRE):
            row_down(k, 0).wait_send()
            row_down(k, 1).wait_send()

    if folded:
        for k in range(1, PRE):

            @pl.when(has_target & (k >= first_passed))
            def _():
                for h in range(2):
                    pass_on(k, h).wait_send()

    @pl.when(has_edge)
    def _():
        for p in range(half - POST, half):
            for j in range(2):
                edge_copy(p, j).wait_send()


def write_out(split, out, sem):
    lanes = split.shape[2]
    pieces = [
        pltpu.make_async_copy(split.at[c], out.at[:, c * lanes : (c + 1) * lanes], sem.at[c])
        for c in range(split.shape[0])
    ]
    for piece in pieces:
        piece.start()
    for piece in pieces:
        piece.wait()


def per_device(n_lat, fields, region, land, coef_table, w_in, b_in, w_mid, b_mid, w_out, b_out):
    n_var, n_lev, n_row, n_lon = fields.shape
    hid = w_in.shape[0]
    pad_lev = -(-n_lev // 16) * 16
    feat = n_var * pad_lev
    rows = n_row + 2 * PRE
    n_split = n_lon // 128
    n_all = n_var * n_lev * n_row
    dma = pltpu.SemaphoreType.DMA
    vmem = pl.BlockSpec(memory_space=pltpu.VMEM)
    hbm = pl.BlockSpec(memory_space=pl.ANY)
    result = pl.pallas_call(
        functools.partial(kernel, n_lat, n_lat == 8, n_var, n_lev, n_row),
        out_shape=pltpu.VMEM((n_split, n_all, 128), F32),
        in_specs=[hbm] * 10,
        out_specs=vmem,
        scratch_shapes=[
            pltpu.VMEM(region.shape, jnp.int32),
            pltpu.VMEM(land.shape, jnp.int32),
            pltpu.VMEM(coef_table.shape[::-1], F32),
            pltpu.VMEM((1, hid), F32),
            pltpu.VMEM(b_mid.shape, F32),
            pltpu.VMEM(b_out.shape, F32),
            pltpu.VMEM(w_in.shape[::-1], BF),
            pltpu.VMEM(w_mid.shape, BF),
            pltpu.VMEM(w_out.shape, BF),
            pltpu.VMEM((hid, 2 * feat), BF),
            pltpu.VMEM((2, feat, hid), BF),
            pltpu.VMEM((n_row, feat, n_lon), BF),
            pltpu.VMEM((2, PRE, feat, n_lon), BF),
            pltpu.VMEM((PRE - 1, feat, n_lon), BF),
            pltpu.VMEM((n_row, n_lon), jnp.int32),
            pltpu.VMEM((2, n_row, n_lon), jnp.int32),
            pltpu.VMEM((rows, feat, n_lon), F32),
            pltpu.VMEM((rows, feat, n_lon), F32),
            pltpu.VMEM((rows, feat, n_lon), F32),
            pltpu.VMEM((rows, feat, n_lon), F32),
            pltpu.VMEM((rows, pad_lev, n_lon), F32),
            pltpu.VMEM((rows, pad_lev, n_lon), F32),
            pltpu.VMEM((rows, pad_lev, n_lon), F32),
            pltpu.VMEM((rows, pad_lev, n_lon), F32),
            pltpu.VMEM((PRE, feat, n_lon), BF),
            pltpu.VMEM((PRE, 2 * feat, n_lon), BF),
            pltpu.VMEM((hid, n_lon), BF),
            pltpu.VMEM((hid, n_lon), BF),
            pltpu.VMEM((PRE, 2, feat, n_lon), BF),
            pltpu.VMEM((n_row + 2 * POST, feat, n_lon), BF),
            pltpu.VMEM((w_mid.shape[0] * hid + 2 * feat, 128), F32),
            dma((n_split,)),
            dma((6,)),
            dma((3,)),
            dma((2,)),
            dma((2,)),
            dma((2, PRE, 2)),
            dma((2, PRE, 2)),
            dma((PRE - 1, 2)),
            dma((PRE - 1, 2)),
            dma((PRE,)),
            dma((PRE,)),
            dma((PRE,)),
            dma((PRE,)),
            dma((POST, 2)),
            dma((2, POST)),
        ],
        compiler_params=pltpu.CompilerParams(
            collective_id=0, has_side_effects=True, vmem_limit_bytes=60 * 2**20
        ),
    )(
        region, land, coef_table.T, b_in.reshape(1, -1), b_mid, b_out,
        fields.reshape(n_all, n_lon), w_in.T, w_mid, w_out,
    )
    closure = pl.pallas_call(
        write_out,
        out_shape=jax.ShapeDtypeStruct((n_all, n_lon), F32),
        in_specs=[vmem],
        out_specs=hbm,
        scratch_shapes=[dma((n_split,))],
    )(pltpu.with_memory_space_constraint(result, pltpu.VMEM))
    return closure.reshape(fields.shape)


def solution(mesh):
    placed = (
        P(None, "lev", ("parts", "lat"), None),
        P(("parts", "lat"), None),
        P(("parts", "lat"), None),
    ) + (P(),) * 7
    return jax.shard_map(
        functools.partial(per_device, mesh.shape["lat"]),
        mesh=mesh,
        in_specs=placed,
        out_specs=P(None, "lev", ("parts", "lat"), None),
        check_vma=False,
    )
```

```python
import functools

import jax
import jax.numpy as jnp
from jax import lax
from jax.experimental import pallas as pl
from jax.experimental.pallas import tpu as pltpu
from jax.sharding import PartitionSpec as P

PRE = 4
POST = 2
PARTS = 3
MESH = pl.DeviceIdType.MESH
BF = jnp.bfloat16
F32 = jnp.float32


SCALE = 0.7978845608028654


def gelu(x):
    inner = x * (SCALE + (SCALE * 0.044715) * (x * x))
    half = 0.5 * x
    return half + half * jnp.tanh(inner)


def gelu_of_half(half):
    inner = half * (2.0 * SCALE + (8.0 * SCALE * 0.044715) * (half * half))
    return half + half * jnp.tanh(inner)


def kernel(
    n_lat, folded, n_var, n_lev, n_row,
    region_hbm, land_hbm, table_hbm, b_in_hbm, b_mid_hbm, b_out_hbm,
    fields, w_in_hbm, w_mid_hbm, w_out_hbm,
    split,
    region, land, table, b_in, b_mid, b_out, w_in, w_mid, w_out, wi, wo,
    sent, halo, passed, edge_passed, code, marks, f0, f1, f2, f3, ef, ew, nf, cf, prof, cols, h1, h2, flux_own, flux, bias,
    in_sem, small_sem, w_sem, mark_send, mark_recv, halo_send, halo_recv, passed_send, passed_recv, prof_send, prof_recv,
    flux_send, flux_recv, edge_send, edge_recv, edge_passed_send, edge_passed_recv,
):
    lat = lax.axis_index("lat")
    lev = lax.axis_index("lev")
    peer = 1 - lev
    has_up = lat > 0
    has_down = lat < n_lat - 1
    odd = lat % 2
    pair = lat // 2
    n_pair = n_lat // 2
    above = pair * (PARTS + 1) // n_pair
    below = (n_pair - 1 - pair) * (PARTS + 1) // n_pair
    first_mine = PARTS - jnp.where(odd == 1, below, above)
    first_passed = PARTS - jnp.where(odd == 1, above, below)
    target = lat + 2 - 4 * odd
    source = lat - 2 + 4 * odd
    has_target = (target >= 0) & (target < n_lat)
    has_source = (source >= 0) & (source < n_lat)
    pad_lev = ef.shape[1]
    feat = n_var * pad_lev
    n_lon = fields.shape[1]
    hid = w_mid.shape[1]
    n_mid = w_mid.shape[0]
    n_region, all_lev = table.shape
    half = n_row // 2
    first = PRE
    last = PRE + n_row - 1

    lanes = split.shape[2]
    n_split = split.shape[0]

    barrier = pltpu.get_barrier_semaphore()
    pl.semaphore_signal(barrier, inc=1, device_id={"lev": peer}, device_id_type=MESH)

    @pl.when(has_up)
    def _():
        for j in range(2):
            pl.semaphore_signal(
                barrier, inc=1, device_id={"lat": lat - 1, "lev": j}, device_id_type=MESH
            )

    @pl.when(has_down)
    def _():
        for j in range(2):
            pl.semaphore_signal(
                barrier, inc=1, device_id={"lat": lat + 1, "lev": j}, device_id_type=MESH
            )

    if folded:

        @pl.when(has_source)
        def _():
            pl.semaphore_signal(barrier, inc=1, device_id={"lat": source}, device_id_type=MESH)

    def columns_of(ref, c):
        return ref.at[:, c * lanes : (c + 1) * lanes]

    pieces = [
        pltpu.make_async_copy(columns_of(fields, c), split.at[c], in_sem.at[c])
        for c in range(n_split)
    ]
    for piece in pieces:
        piece.start()
    small = [
        pltpu.make_async_copy(source, target, small_sem.at[k])
        for k, (source, target) in enumerate((
            (region_hbm, region), (land_hbm, land), (table_hbm, table),
            (b_in_hbm, b_in), (b_mid_hbm, b_mid), (b_out_hbm, b_out),
        ))
    ]
    for piece in small:
        piece.start()
    loads = [
        pltpu.make_async_copy(w_in_hbm, w_in, w_sem.at[0]),
        pltpu.make_async_copy(w_out_hbm, w_out, w_sem.at[1]),
        pltpu.make_async_copy(w_mid_hbm, w_mid, w_sem.at[2]),
    ]

    def take_row(r):
        for v in range(n_var):
            base = v * n_lev * n_row
            values = jnp.concatenate(
                [split[c, pl.ds(base + r, n_lev, stride=n_row), :] for c in range(n_split)],
                axis=1,
            )
            values = jnp.concatenate(
                [values, jnp.ones((pad_lev - n_lev, n_lon), F32)], axis=0
            )
            f0[PRE + r, v * pad_lev : (v + 1) * pad_lev, :] = values
            sent[r, v * pad_lev : (v + 1) * pad_lev, :] = values.astype(BF)

    step = feat // 16 // PARTS * 16
    big = feat - (PARTS - 1) * step

    def part_of(h):
        return pl.ds(0, big) if h == 0 else pl.ds(big + (h - 1) * step, step)

    def row_up(k, h):
        part = part_of(h)
        return pltpu.make_async_remote_copy(
            src_ref=sent.at[k, part], dst_ref=halo.at[1, k, part],
            send_sem=halo_send.at[1, k, h], recv_sem=halo_recv.at[1, k, h],
            device_id={"lat": lat - 1}, device_id_type=MESH,
        )

    def row_down(k, h):
        part = part_of(h)
        return pltpu.make_async_remote_copy(
            src_ref=sent.at[n_row - 1 - k, part], dst_ref=halo.at[0, k, part],
            send_sem=halo_send.at[0, k, h], recv_sem=halo_recv.at[0, k, h],
            device_id={"lat": lat + 1}, device_id_type=MESH,
        )

    def by_pair(side, h):
        return (odd == 1 - side) & (h >= first_mine) if folded else lat < 0

    def to_pair(side, k, h):
        part = part_of(h)
        row = n_row - 1 - k if side == 0 else k
        return pltpu.make_async_remote_copy(
            src_ref=sent.at[row, part], dst_ref=passed.at[k - 1, part],
            send_sem=halo_send.at[side, k, h], recv_sem=passed_recv.at[k - 1, h],
            device_id={"lat": lat + 1 - 2 * odd}, device_id_type=MESH,
        )

    def pass_on(k, h):
        part = part_of(h)
        return pltpu.make_async_remote_copy(
            src_ref=passed.at[k - 1, part], dst_ref=halo.at[odd, k, part],
            send_sem=passed_send.at[k - 1, h], recv_sem=halo_recv.at[odd, k, h],
            device_id={"lat": target}, device_id_type=MESH,
        )

    def send_row(side, k, h):
        exists, row = ((has_down, row_down), (has_up, row_up))[side]

        @pl.when(exists & jnp.logical_not(by_pair(side, h)))
        def _():
            row(k, h).start()

    def send_pair(side, k):
        if folded:
            exists = (has_down, has_up)[side]
            for h in range(PARTS):

                @pl.when(exists & by_pair(side, h))
                def _():
                    to_pair(side, k, h).start()

    def marks_to(side, target):
        part = pl.ds(0, PRE) if side == 1 else pl.ds(n_row - PRE, PRE)
        return pltpu.make_async_remote_copy(
            src_ref=code.at[part], dst_ref=marks.at[side, part],
            send_sem=mark_send.at[side], recv_sem=mark_recv.at[side],
            device_id={"lat": target}, device_id_type=MESH,
        )

    for piece in pieces + small:
        piece.wait()
    code[...] = region[...] + n_region * land[...]
    take_row(0)
    take_row(n_row - 1)
    for load in loads:
        load.start()

    greeted = 1 + 2 * has_up.astype(jnp.int32) + 2 * has_down.astype(jnp.int32)
    if folded:
        greeted = greeted + has_target.astype(jnp.int32)
    pl.semaphore_wait(barrier, greeted)

    @pl.when(has_up)
    def _():
        marks_to(1, lat - 1).start()
        for h in range(PARTS):
            row_up(0, h).start()

    @pl.when(has_down)
    def _():
        marks_to(0, lat + 1).start()
        for h in range(PARTS):
            row_down(0, h).start()

    for k in range(1, PRE):
        take_row(k)
        take_row(n_row - 1 - k)
        if k == 1:
            send_pair(1, 1)
            send_pair(0, 1)

    wide = jnp.concatenate([table[...], jnp.zeros((n_region, 128 - all_lev), F32)], axis=1)
    wide = pltpu.roll(wide, (128 - lev * n_lev) % 128, 1)
    wide = jnp.concatenate([wide] * (128 // n_region), axis=0).T[:pad_lev]
    level_id = lax.broadcasted_iota(jnp.int32, (pad_lev, 128), 0)
    wide = jnp.where(level_id < n_lev, wide, 0.0)
    columns = [
        jnp.broadcast_to(wide[:, k : k + 1], (pad_lev, n_lon)) for k in range(n_region)
    ]

    def coefficient(region_row, land_row):
        region_row = jnp.broadcast_to(region_row, (pad_lev, n_lon))
        total = columns[0]
        for k in range(1, len(columns)):
            total = jnp.where(region_row == k, columns[k], total)
        return total * (1.0 - 0.6 * land_row.astype(F32))

    for r in range(n_row):
        ef[first + r] = coefficient(region[r : r + 1, :], land[r : r + 1, :])

    def faces_north(i):
        nf[i] = jnp.sqrt(ef[i] * ef[i + 1])

    def faces_east(i):
        c = ef[i]
        east = jnp.sqrt(c * pltpu.roll(c, n_lon - 1, 1))
        ef[i] = east
        ew[i] = pltpu.roll(east, 1, 1)

    for i in range(first, last):
        faces_north(i)

    def centre(i):
        cf[i] = 1.0 - ((ef[i] + ew[i]) + (nf[i] + nf[i - 1]))

    def step_rows(src, dst, i, store=None):
        size = 16
        for s in range(0, pad_lev, size):
            own = cf[i, s : s + size, :]
            east = ef[i, s : s + size, :]
            west = ew[i, s : s + size, :]
            north = nf[i, s : s + size, :]
            south = nf[i - 1, s : s + size, :]
            for v in range(n_var):
                rows = slice(v * pad_lev + s, v * pad_lev + s + size)
                f = src[i, rows, :]
                near = f.astype(BF)
                zonal = east * pltpu.roll(near, n_lon - 1, 1).astype(F32)
                zonal = zonal + west * pltpu.roll(near, 1, 1).astype(F32)
                meridional = north * src[i + 1, rows, :] + south * src[i - 1, rows, :]
                value = (own * f + zonal) + meridional
                if store is None:
                    dst[i, rows, :] = value
                else:
                    store(v, s, rows, value)

    def loop_rows(low, high, fn):
        def body(i, carry):
            fn(i)
            return carry

        lax.fori_loop(low, high, body, 0)

    for side in range(2):
        exists = has_up if side == 0 else has_down

        @pl.when(exists)
        def _():
            marks_to(side, lat - 1 + 2 * side).wait_recv()
            for k in range(PRE):
                r = n_row - 1 - k if side == 0 else k
                i = first - 1 - k if side == 0 else last + 1 + k
                mark = marks[side, r : r + 1, :]
                is_land = jnp.where(mark >= n_region, 1, 0)
                ef[i] = coefficient(mark - n_region * is_land, is_land)

        @pl.when(jnp.logical_not(exists))
        def _():
            for k in range(PRE):
                i = first - 1 - k if side == 0 else last + 1 + k
                ef[i] = jnp.zeros((pad_lev, n_lon), F32)
                f0[i] = jnp.zeros((feat, n_lon), F32)

    for i in list(range(0, first)) + list(range(last, last + PRE)):
        faces_north(i)
    for i in range(0, last + PRE + 1):
        faces_east(i)
    for i in range(1, last + PRE):
        centre(i)

    send_row(1, 1, 0)
    send_row(0, 1, 0)

    loop_rows(first + 1, last, lambda i: step_rows(f0, f1, i))
    loop_rows(first + 2, last - 1, lambda i: step_rows(f1, f2, i))
    loop_rows(first + 3, last - 2, lambda i: step_rows(f2, f3, i))

    loads[0].wait()
    loads[1].wait()
    n_feat = w_out.shape[0]
    f_id = lax.broadcasted_iota(jnp.int32, (feat, n_feat), 1)
    c_id = lax.broadcasted_iota(jnp.int32, (feat, n_feat), 0)
    l_id = c_id % pad_lev
    half_b = 0.5 * b_in[...]
    b_parts = []
    for _ in range(3):
        b_parts.append(half_b.astype(BF))
        half_b = half_b - b_parts[-1].astype(F32)
    place_id = lax.broadcasted_iota(jnp.int32, (feat, hid), 0)
    for j in range(2):
        want = (c_id // pad_lev) * (2 * n_lev) + j * n_lev + l_id
        found = (f_id == want) & (l_id < n_lev)
        halves = jnp.where(found, 0.5, 0.0).astype(BF)
        weight = jnp.dot(halves, w_in[...], preferred_element_type=F32)
        if j == 0:
            for place, part in zip((n_lev, n_lev + 1, pad_lev + n_lev), b_parts):
                weight = jnp.where(place_id == place, part.astype(F32), weight)
        wi[:, j * feat : (j + 1) * feat] = weight.T.astype(BF)
        pick = jnp.where(found, 1.0, 0.0).astype(BF)
        wo[j] = jnp.dot(pick, w_out[...], preferred_element_type=F32).astype(BF)

    def tall(row):
        return jnp.broadcast_to(row, (128, 128)).T

    start = n_mid * hid
    for m in range(0, n_feat, 128):
        count = min(128, n_feat - m)
        row = b_out[m : m + count].reshape(1, count)
        if count < 128:
            row = jnp.concatenate([row, jnp.zeros((1, 128 - count), F32)], axis=1)
        bias[m : m + 128, :] = tall(row)
    bias[start : start + 2 * feat, :] = jnp.zeros((2 * feat, 128), F32)
    for v in range(n_var):
        for j in range(2):
            place = start + j * feat + v * pad_lev
            origin = v * 2 * n_lev + j * n_lev
            bias[place : place + n_lev, :] = bias[origin : origin + n_lev, :]
    for m in range(0, hid, 128):
        for layer in range(n_mid):
            start = layer * hid + m
            bias[start : start + 128, :] = tall(b_mid[layer : layer + 1, m : m + 128])
    loads[2].wait()

    tile = 256

    def with_bias(x, start, size):
        b = bias[start : start + size, :]
        return x + jnp.concatenate([b] * (n_lon // b.shape[1]), axis=1)

    def profile_copy(p):
        return pltpu.make_async_remote_copy(
            src_ref=prof.at[p], dst_ref=cols.at[p, pl.ds(lev * feat, feat)],
            send_sem=prof_send.at[p], recv_sem=prof_recv.at[p],
            device_id={"lev": peer}, device_id_type=MESH,
        )

    def flux_row(owner, p):
        return half - 1 - p + owner * (1 + 2 * p)

    def flux_copy(p):
        return pltpu.make_async_remote_copy(
            src_ref=flux_own.at[p, peer], dst_ref=flux.at[flux_row(lev, p) + POST],
            send_sem=flux_send.at[p], recv_sem=flux_recv.at[p],
            device_id={"lev": peer}, device_id_type=MESH,
        )

    def edge_copy(p, j, h):
        q = p - (half - POST)
        place = flux_row(lev, p) + POST + (1 - 2 * lev) * n_row
        return pltpu.make_async_remote_copy(
            src_ref=flux_own.at[p, j, part_of(h)], dst_ref=flux.at[place, part_of(h)],
            send_sem=edge_send.at[q, j, h], recv_sem=edge_recv.at[peer, q, h],
            device_id={"lat": lat - 1 + 2 * lev, "lev": j}, device_id_type=MESH,
        )

    def edge_to_pair(j, h):
        return pltpu.make_async_remote_copy(
            src_ref=flux_own.at[half - POST, j, part_of(h)], dst_ref=edge_passed.at[part_of(h)],
            send_sem=edge_send.at[0, j, h], recv_sem=edge_passed_recv.at[h],
            device_id={"lat": lat + 1 - 2 * odd, "lev": j}, device_id_type=MESH,
        )

    def edge_on(h):
        p = half - POST
        place = jnp.where(
            odd == 1, flux_row(0, p) + POST + n_row, flux_row(1, p) + POST - n_row
        )
        return pltpu.make_async_remote_copy(
            src_ref=edge_passed.at[part_of(h)], dst_ref=flux.at[place, part_of(h)],
            send_sem=edge_passed_send.at[h], recv_sem=edge_recv.at[odd, 0, h],
            device_id={"lat": target}, device_id_type=MESH,
        )

    def edge_by_pair(h):
        return (lev == odd) & (h >= first_mine) if folded else lat < 0

    def send_edge(p, j):
        for h in range(PARTS):

            @pl.when(has_edge & jnp.logical_not((p == half - POST) & edge_by_pair(h)))
            def _():
                edge_copy(p, j, h).start()

    has_edge = jnp.where(lev == 0, has_up, has_down)

    def smooth(p, side, store):
        @pl.when(jnp.where(side == 0, has_up, has_down))
        def _():
            for h in range(PARTS):
                part = part_of(h)
                pltpu.make_async_remote_copy(
                    src_ref=sent.at[0, part], dst_ref=halo.at[side, p, part],
                    send_sem=halo_send.at[side, p, h], recv_sem=halo_recv.at[side, p, h],
                    device_id={"lev": peer}, device_id_type=MESH,
                ).wait_recv()
            f0[jnp.where(side == 0, first - 1 - p, last + 1 + p)] = halo[side, p].astype(F32)

        for k, (src, dst) in enumerate(((f0, f1), (f1, f2), (f2, f3), (f3, None))):
            at = jnp.where(side == 0, first - p + k, last + p - k)
            step_rows(src, dst, at, store if dst is None else None)

    def phase(p, carry):
        def save_peer(v, s, rows, value):
            prof[p, rows, :] = value.astype(BF)

        def save_own(v, s, rows, value):
            place = pl.multiple_of(lev * feat + rows.start, 16)
            cols[p, pl.ds(place, rows.stop - rows.start), :] = value.astype(BF)

        smooth(p, peer, save_peer)
        exchange = profile_copy(p)
        exchange.start()
        smooth(p, lev, save_own)

        @pl.when(p < PRE - 1)
        def _():
            for side in (1, 0):
                for h in range(1, PARTS):
                    send_row(side, p + 1, h)

        @pl.when(p < PRE - 2)
        def _():
            for side in (1, 0):
                send_pair(side, p + 2)

        @pl.when(p > half - POST)
        def _():
            send_edge(p - 1, 1)

        if folded:
            for h in range(PARTS):

                @pl.when(has_target & (p < PRE - 1) & (h >= first_passed))
                def _():
                    to_pair(0, p + 1, h).wait_recv()
                    pass_on(p + 1, h).start()

        pltpu.make_async_remote_copy(
            src_ref=prof.at[p], dst_ref=cols.at[p, pl.ds(peer * feat, feat)],
            send_sem=prof_send.at[p], recv_sem=prof_recv.at[p],
            device_id={"lev": peer}, device_id_type=MESH,
        ).wait_recv()

        for m in range(0, hid, tile):
            x = jnp.dot(wi[m : m + tile, :], cols[p], preferred_element_type=F32)
            h1[m : m + tile, :] = gelu_of_half(x).astype(BF)
        now, then = h1, h2
        for layer in range(n_mid):
            for m in range(0, hid, tile):
                x = jnp.dot(w_mid[layer, m : m + tile, :], now[...], preferred_element_type=F32)
                x = with_bias(x, layer * hid + m, tile)
                then[m : m + tile, :] = gelu(x).astype(BF)
            now, then = then, now
        for j in range(2):
            x = jnp.dot(wo[j], now[...], preferred_element_type=F32)
            flux_own[p, j] = with_bias(x, n_mid * hid + j * feat, feat).astype(BF)
        @pl.when(p < PRE - 2)
        def _():
            for side in (1, 0):
                send_row(side, p + 2, 0)

        flux[flux_row(lev, p) + POST] = flux_own[p, lev]
        flux_copy(p).start()

        if folded:

            @pl.when(has_edge & (p == half - POST))
            def _():
                for h in range(PARTS):

                    @pl.when(edge_by_pair(h))
                    def _():
                        for j in range(2):
                            edge_to_pair(j, h).start()

        @pl.when(p >= half - POST)
        def _():
            send_edge(p, 0)

        return carry

    lax.fori_loop(0, PRE, phase, 0)

    send_edge(half - 1, 1)
    if folded:
        for h in range(PARTS):

            @pl.when(has_target & (h >= first_passed))
            def _():
                edge_to_pair(0, h).wait_recv()
                edge_on(h).start()

    for p in range(half):
        flux_copy(p).wait_recv()

    def widen(i):
        f0[i] = flux[i - PRE + POST].astype(F32)

    loop_rows(first, last + 1, widen)

    def finish(i):
        def store(v, s, rows, value):
            count = min(16, n_lev - s)
            base = v * (n_lev * n_row) + s * n_row + (i - first)
            for c in range(n_split):
                split[c, pl.ds(base, count, stride=n_row), :] = value[
                    :count, c * lanes : (c + 1) * lanes
                ]

        step_rows(f1, None, i, store)

    loop_rows(first + 1, last, lambda i: step_rows(f0, f1, i))
    loop_rows(first + 2, last - 1, finish)

    for side in range(2):
        exists = has_up if side == 0 else has_down

        @pl.when(exists)
        def _():
            for q in range(POST):
                place = n_row + 2 * POST - 1 - q if side == 1 else q
                for h in range(PARTS):
                    pltpu.make_async_remote_copy(
                        src_ref=flux_own.at[0, 0, part_of(h)],
                        dst_ref=flux.at[place, part_of(h)],
                        send_sem=edge_send.at[0, 0, h], recv_sem=edge_recv.at[side, q, h],
                        device_id={"lev": peer}, device_id_type=MESH,
                    ).wait_recv()
            for q in range(POST):
                widen(first - 1 - q if side == 0 else last + 1 + q)

    for i in (first - 1, first, last, last + 1):
        step_rows(f0, f1, i)
    for i in (first, first + 1, last - 1, last):
        finish(i)
    for k in range(PRE):
        profile_copy(k).wait_send()
        flux_copy(k).wait_send()

    @pl.when(has_up)
    def _():
        marks_to(1, lat - 1).wait_send()
        for k in range(PRE):
            for h in range(PARTS):
                row_up(k, h).wait_send()

    @pl.when(has_down)
    def _():
        marks_to(0, lat + 1).wait_send()
        for k in range(PRE):
            for h in range(PARTS):
                row_down(k, h).wait_send()

    if folded:
        for h in range(PARTS):

            @pl.when(has_target & (h >= first_passed))
            def _():
                for k in range(1, PRE):
                    pass_on(k, h).wait_send()
                edge_on(h).wait_send()

    @pl.when(has_edge)
    def _():
        for p in range(half - POST, half):
            for j in range(2):
                for h in range(PARTS):
                    edge_copy(p, j, h).wait_send()


def write_out(split, out, sem):
    lanes = split.shape[2]
    pieces = [
        pltpu.make_async_copy(split.at[c], out.at[:, c * lanes : (c + 1) * lanes], sem.at[c])
        for c in range(split.shape[0])
    ]
    for piece in pieces:
        piece.start()
    for piece in pieces:
        piece.wait()


def per_device(n_lat, fields, region, land, coef_table, w_in, b_in, w_mid, b_mid, w_out, b_out):
    n_var, n_lev, n_row, n_lon = fields.shape
    hid = w_in.shape[0]
    pad_lev = -(-n_lev // 16) * 16
    feat = n_var * pad_lev
    rows = n_row + 2 * PRE
    n_split = n_lon // 128
    n_all = n_var * n_lev * n_row
    dma = pltpu.SemaphoreType.DMA
    vmem = pl.BlockSpec(memory_space=pltpu.VMEM)
    hbm = pl.BlockSpec(memory_space=pl.ANY)
    result = pl.pallas_call(
        functools.partial(kernel, n_lat, n_lat == 8, n_var, n_lev, n_row),
        out_shape=pltpu.VMEM((n_split, n_all, 128), F32),
        in_specs=[hbm] * 10,
        out_specs=vmem,
        scratch_shapes=[
            pltpu.VMEM(region.shape, jnp.int32),
            pltpu.VMEM(land.shape, jnp.int32),
            pltpu.VMEM(coef_table.shape[::-1], F32),
            pltpu.VMEM((1, hid), F32),
            pltpu.VMEM(b_mid.shape, F32),
            pltpu.VMEM(b_out.shape, F32),
            pltpu.VMEM(w_in.shape[::-1], BF),
            pltpu.VMEM(w_mid.shape, BF),
            pltpu.VMEM(w_out.shape, BF),
            pltpu.VMEM((hid, 2 * feat), BF),
            pltpu.VMEM((2, feat, hid), BF),
            pltpu.VMEM((n_row, feat, n_lon), BF),
            pltpu.VMEM((2, PRE, feat, n_lon), BF),
            pltpu.VMEM((PRE - 1, feat, n_lon), BF),
            pltpu.VMEM((feat, n_lon), BF),
            pltpu.VMEM((n_row, n_lon), jnp.int32),
            pltpu.VMEM((2, n_row, n_lon), jnp.int32),
            pltpu.VMEM((rows, feat, n_lon), F32),
            pltpu.VMEM((rows, feat, n_lon), F32),
            pltpu.VMEM((rows, feat, n_lon), F32),
            pltpu.VMEM((rows, feat, n_lon), F32),
            pltpu.VMEM((rows, pad_lev, n_lon), F32),
            pltpu.VMEM((rows, pad_lev, n_lon), F32),
            pltpu.VMEM((rows, pad_lev, n_lon), F32),
            pltpu.VMEM((rows, pad_lev, n_lon), F32),
            pltpu.VMEM((PRE, feat, n_lon), BF),
            pltpu.VMEM((PRE, 2 * feat, n_lon), BF),
            pltpu.VMEM((hid, n_lon), BF),
            pltpu.VMEM((hid, n_lon), BF),
            pltpu.VMEM((PRE, 2, feat, n_lon), BF),
            pltpu.VMEM((n_row + 2 * POST, feat, n_lon), BF),
            pltpu.VMEM((w_mid.shape[0] * hid + 2 * feat, 128), F32),
            dma((n_split,)),
            dma((6,)),
            dma((3,)),
            dma((2,)),
            dma((2,)),
            dma((2, PRE, PARTS)),
            dma((2, PRE, PARTS)),
            dma((PRE - 1, PARTS)),
            dma((PRE - 1, PARTS)),
            dma((PRE,)),
            dma((PRE,)),
            dma((PRE,)),
            dma((PRE,)),
            dma((POST, 2, PARTS)),
            dma((2, POST, PARTS)),
            dma((PARTS,)),
            dma((PARTS,)),
        ],
        compiler_params=pltpu.CompilerParams(
            collective_id=0, has_side_effects=True, vmem_limit_bytes=60 * 2**20
        ),
    )(
        region, land, coef_table.T, b_in.reshape(1, -1), b_mid, b_out,
        fields.reshape(n_all, n_lon), w_in.T, w_mid, w_out,
    )
    closure = pl.pallas_call(
        write_out,
        out_shape=jax.ShapeDtypeStruct((n_all, n_lon), F32),
        in_specs=[vmem],
        out_specs=hbm,
        scratch_shapes=[dma((n_split,))],
    )(pltpu.with_memory_space_constraint(result, pltpu.VMEM))
    return closure.reshape(fields.shape)


def solution(mesh):
    placed = (
        P(None, "lev", ("parts", "lat"), None),
        P(("parts", "lat"), None),
        P(("parts", "lat"), None),
    ) + (P(),) * 7
    return jax.shard_map(
        functools.partial(per_device, mesh.shape["lat"]),
        mesh=mesh,
        in_specs=placed,
        out_specs=P(None, "lev", ("parts", "lat"), None),
        check_vma=False,
    )
```
